256 devices in a mesh: dom: 32 (over x, z_hi, y), mode: 8 (over z_lo, core).
Axes of the slice: x: 4, y: 4, z: 8 (z_hi: 2, z_lo: 4; z = z_hi * 4 + z_lo), core: 2. Of those that a mesh axis runs over, the one named last changes fastest.
Arguments:
- iterate: float32 [256, 1024, 256], P('mode', 'dom'), may hold values from -6 to 6
- source: float32 [256, 1024, 256], P('mode', 'dom'), may hold values from -6 to 6
- mean_coef: float32 [1024, 256], P('dom'), may hold values from 0.5 to 2
- kl_fields: float32 [20, 1024, 256], P(None, 'dom'), may hold values from -1 to 1
- tri_index: int32 [5376, 3], replicated, may hold values from 0 to 255, as said below
- tri_value: float32 [5376], replicated, may hold values from 0.25 to 1.75, as said below
Outputs:
- updated: float32 [256, 1024, 256], P('mode', 'dom')
- residual: float32 [256, 1024, 256], P('mode', 'dom')
The draws below stay inside these ranges and needn't reach their ends.
Inputs may be any that keep to these rules, and one draw needn't show every extreme that they name: `tri_index`: every pair of a mode i and a field l appears in exactly one entry; entries of field 0 have j = i; for fields 1 to 20 the entry (i, j, l) is listed together with (j, i, l), j differing from i; rows stand in a random order. `tri_value`: the entries (i, j, l) and (j, i, l) carry the same value.
All inputs are finite; a program needn't handle non-finite values.
Results may differ from the reference program's by a relative error of at most 0.0062.
Values may be sent and summed in bfloat16 or wider, within the bound.
A program may use at most 64 MiB of HBM per device.

```python
import math
import jax
import jax.numpy as jnp
from jax import lax

P_SIZE = 256
L = 20
NY = 16
NZ = 16
NX = 1024


def pairing_tables(key):
    partners = []
    slots = []
    for level in range(1, L + 1):
        order = jax.random.permutation(jax.random.fold_in(key, 1000 + level), P_SIZE).astype(jnp.int32)
        place = jnp.argsort(order).astype(jnp.int32)
        partners.append(order[place ^ 1])
        slots.append(place // 2)
    row_order = jax.random.permutation(jax.random.fold_in(key, 77), P_SIZE * (L + 1)).astype(jnp.int32)
    return (jnp.stack(partners), jnp.stack(slots), row_order)


def draw_tri_index(key, part):
    partners, slots, row_order = pairing_tables(key)
    modes = jnp.arange(P_SIZE, dtype=jnp.int32)
    blocks = [jnp.stack([modes, modes, jnp.zeros_like(modes)], 1)]
    for level in range(1, L + 1):
        blocks.append(jnp.stack([modes, partners[level - 1], jnp.full_like(modes, level)], 1))
    listing = jnp.concatenate(blocks, 0)
    return listing[row_order]


def draw_tri_value(key, part):
    partners, slots, row_order = pairing_tables(key)
    low_end, high_end = (0.5, 1.5)
    diagonal = jax.random.uniform(jax.random.fold_in(key, 2000), (P_SIZE,), jnp.float32, low_end, high_end)
    paired = jax.random.uniform(jax.random.fold_in(key, 2001), (L, P_SIZE // 2), jnp.float32, low_end, high_end)
    blocks = [diagonal]
    for level in range(1, L + 1):
        blocks.append(paired[level - 1][slots[level - 1]])
    listing = jnp.concatenate(blocks, 0)
    return listing[row_order]


def block_levels(rng, dims, cuts, low, largest):
    def one(dim, shards_of):
        draws = jax.random.uniform(jax.random.fold_in(jax.random.fold_in(rng, 6), dim), (shards_of,), jnp.float32, low / len(cuts), largest / len(cuts))
        return jnp.repeat(jnp.exp(draws), dims[dim] // shards_of).reshape((-1,) + (1,) * (len(dims) - dim - 1))

    gain = one(*cuts[0])
    for cut in cuts[1:]:
        gain = gain * one(*cut)
    return gain


def scatter_about(rng, extent, width, bound, pieces=(), held_as=jnp.bfloat16):
    values = jax.random.normal(rng, extent, jnp.float32) * width
    if len(pieces) > 0:
        values = block_levels(rng, extent, pieces, -0.22, 0.18) * values
    return jnp.clip(values, min=-bound, max=bound).astype(held_as)


def setup_inputs(seed: int = 0) -> dict:
    splits = jax.random.split(jax.random.key(seed), 7)
    return {
        "iterate": scatter_about(splits[0], (P_SIZE, NX, NY * NZ), 1.0, 6.0, ((0, 8), (1, 32)), jnp.float32),
        "source": scatter_about(splits[1], (P_SIZE, NX, NY * NZ), 1.0, 6.0, ((0, 8), (1, 32)), jnp.float32),
        "mean_coef": jnp.clip(jnp.exp(math.log(2.0) - 1.3862944 * jax.random.uniform(splits[2], (NX, NY * NZ), jnp.float32) ** block_levels(splits[2], (NX, NY * NZ), ((0, 32),), -0.2, 0.2)), 0.5, 2.0),
        "kl_fields": scatter_about(splits[3], (L, NX, NY * NZ), 0.25, 1.0, ((1, 32),), jnp.float32),
        "tri_index": draw_tri_index(jax.random.fold_in(splits[6], 71), 0),
        "tri_value": draw_tri_value(jax.random.fold_in(splits[6], 71), 0),
    }


cheb_center = 1.125
cheb_radius = 0.875


def shifted(field, offset):
    if offset > 0:
        filler = jnp.zeros(field.shape[:-1] + (offset,), field.dtype)
        return jnp.concatenate([field[..., offset:], filler], -1)
    amount = -offset
    filler = jnp.zeros(field.shape[:-1] + (amount,), field.dtype)
    return jnp.concatenate([filler, field[..., :-amount]], -1)


def z_masks(cells, z_depth):
    z_place = jnp.arange(cells) % z_depth
    return (z_place < z_depth - 1).astype(jnp.float32), (z_place > 0).astype(jnp.float32)


def face_weights(padded_coef, upper_mask, lower_mask, z_depth):
    centre = padded_coef[:, 1:-1]
    return (0.5 * (centre + padded_coef[:, 2:]),
            0.5 * (centre + padded_coef[:, :-2]),
            0.5 * (centre + shifted(centre, z_depth)),
            0.5 * (centre + shifted(centre, -z_depth)),
            0.5 * (centre + shifted(centre, 1) * upper_mask),
            0.5 * (centre + shifted(centre, -1) * lower_mask))


def apply_stencil(padded, face_set, upper_mask, lower_mask, z_depth):
    centre = padded[:, 1:-1]
    result = face_set[0] * (centre - padded[:, 2:]) + face_set[1] * (centre - padded[:, :-2])
    result = result + face_set[2] * (centre - shifted(centre, z_depth)) + face_set[3] * (centre - shifted(centre, -z_depth))
    result = result + face_set[4] * (centre - shifted(centre, 1) * upper_mask)
    return result + face_set[5] * (centre - shifted(centre, -1) * lower_mask)


def reference(iterate, source, mean_coef, kl_fields, tri_index, tri_value):
    cells = NY * NZ
    coef = jnp.concatenate([mean_coef[None], kl_fields], 0)
    padded_coef = jnp.pad(coef, ((0, 0), (1, 1), (0, 0)))
    upper_mask, lower_mask = z_masks(cells, NZ)
    face_set = face_weights(padded_coef, upper_mask, lower_mask, NZ)
    dense = jnp.zeros((P_SIZE, L + 1, P_SIZE), jnp.float32)
    dense = dense.at[tri_index[:, 0], tri_index[:, 2], tri_index[:, 1]].add(tri_value)
    dense = dense.astype(jnp.bfloat16).astype(jnp.float32)
    matrices = jnp.transpose(dense, (1, 0, 2))
    rounded = iterate.astype(jnp.bfloat16).astype(jnp.float32)
    flat = jnp.pad(rounded, ((0, 0), (1, 1), (0, 0))).reshape(P_SIZE, -1)

    def accumulate(total, items):
        matrix, faces_here = items
        mixed = jnp.dot(matrix, flat, precision=lax.Precision.HIGHEST).reshape(P_SIZE, NX + 2, cells)
        return total + apply_stencil(mixed, faces_here, upper_mask, lower_mask, NZ), None

    image, _ = lax.scan(accumulate, jnp.zeros((P_SIZE, NX, cells), jnp.float32), (matrices, face_set))
    residual = source - image
    mean_faces = tuple(weight[0] for weight in face_set)
    diag = mean_faces[0] + mean_faces[1] + mean_faces[2] + mean_faces[3] + mean_faces[4] + mean_faces[5]
    sigma = cheb_center / cheb_radius
    rho_zero = 1.0 / sigma
    rho_one = 1.0 / (2.0 * sigma - rho_zero)
    first = residual / (cheb_center * diag)
    padded_first = jnp.pad(first, ((0, 0), (1, 1), (0, 0)))
    smoothed = residual - apply_stencil(padded_first, mean_faces, upper_mask, lower_mask, NZ)
    second = rho_one * rho_zero * first + (2.0 * rho_one / cheb_radius) * smoothed / diag
    return iterate + first + second, residual
```

```python
import jax
import jax.numpy as jnp
from jax import lax
from jax.experimental import pallas as pl
from jax.experimental.pallas import tpu as pltpu
from jax.sharding import PartitionSpec as P

P_SIZE = 256
NF = 21
NZ = 16
CELLS = 256
IB = 32
NIB = P_SIZE // IB
ENTRIES = P_SIZE * NF

cheb_center = 1.125
cheb_radius = 0.875
sigma = cheb_center / cheb_radius
rho_zero = 1.0 / sigma
rho_one = 1.0 / (2.0 * sigma - rho_zero)

f32 = jnp.float32
bf16 = jnp.bfloat16
i32 = jnp.int32


def iota(shape, dim):
    return lax.broadcasted_iota(i32, shape, dim)


def plane_neighbours():
    q = iota((CELLS, CELLS), 0)
    p = iota((CELLS, CELLS), 1)
    far = jnp.abs(q - p)
    same = (q >> 4) == (p >> 4)
    return jnp.where((far == NZ) | ((far == 1) & same), 1.0, 0.0).astype(bf16)


def build_mixing(tri_ref, val_ref, mix_ref, table_ref):
    mode = iota((P_SIZE, 256), 0)
    level = iota((32, 256), 0)

    def gather(step, total):
        here = pl.ds(pl.multiple_of(step * 256, 256), 256)
        hot = jnp.where(mode == tri_ref[0:1, here], 1.0, 0.0).astype(bf16)
        mine = level == tri_ref[2:3, here]
        coef = jnp.where(mine, val_ref[0:1, here], 0.0).astype(bf16)
        trial = jnp.where(mine, tri_ref[1:2, here].astype(f32), 0.0).astype(bf16)
        both = jnp.concatenate([coef, trial], 0)
        return total + lax.dot_general(
            hot, both, (((1,), (1,)), ((), ())), preferred_element_type=f32
        )

    table_ref[...] = lax.fori_loop(0, ENTRIES // 256, gather, jnp.zeros((P_SIZE, 64), f32))
    column = iota((P_SIZE, P_SIZE), 1).astype(f32)
    for l in range(NF):
        coef = table_ref[:, l : l + 1]
        trial = table_ref[:, 32 + l : 33 + l]
        panel = jnp.where(column == trial, coef, 0.0).astype(bf16)
        mix_ref[:, l * IB : (l + 1) * IB, :] = panel.reshape(NIB, IB, P_SIZE)


def swap_matrix(major, minor):
    n = major * minor
    r = iota((n, n), 0)
    c = iota((n, n), 1)
    shift = minor.bit_length() - 1
    wanted = (r & (minor - 1)) * major + (r >> shift)
    return jnp.where(c == wanted, 1.0, 0.0).astype(bf16)


def prepare_kernel(tri_ref, val_ref, it_ref, mix_ref, rows_ref, table_ref):
    swap = swap_matrix(32, 16)
    for g in range(2):
        block = it_ref[16 * g : 16 * (g + 1)].astype(bf16).reshape(512, CELLS)
        turned = jnp.dot(swap, block, preferred_element_type=f32).astype(bf16)
        rows_ref[:, 16 * g : 16 * (g + 1), :] = turned.reshape(32, 16, CELLS)
    build_mixing(tri_ref, val_ref, mix_ref, table_ref)


def lane_neighbours(x, z_place, place):
    up = jnp.where(z_place < NZ - 1, pltpu.roll(x, CELLS - 1, x.ndim - 1), 0.0)
    down = jnp.where(z_place > 0, pltpu.roll(x, 1, x.ndim - 1), 0.0)
    far = jnp.where(place < CELLS - NZ, pltpu.roll(x, CELLS - NZ, x.ndim - 1), 0.0)
    near = jnp.where(place >= NZ, pltpu.roll(x, NZ, x.ndim - 1), 0.0)
    return up + down + far + near


def image_kernel(r_ref, mix_ref, b_ref, out_ref, g_ref, nb_ref, s_ref, t_ref):
    near = plane_neighbours()
    place = iota((24, CELLS), 1)
    for x in range(4):
        nb_ref[x] = b_ref[x] + b_ref[x + 2] + lane_neighbours(b_ref[x + 1], place & (NZ - 1), place)
        own = r_ref[x + 1]
        around = jnp.dot(own, near, preferred_element_type=f32)
        g = 6.0 * own.astype(f32) - around - r_ref[x].astype(f32) - r_ref[x + 2].astype(f32)
        g_ref[x] = g.astype(bf16)

    def block(ib, _):
        rows = pl.ds(pl.multiple_of(ib * IB, IB), IB)
        for s in range(6):
            u = jnp.dot(mix_ref[ib], r_ref[s], preferred_element_type=f32).reshape(NF, IB, CELLS)
            total = b_ref[s, 0:1] * u[0]
            for l in range(1, NF):
                total = total + b_ref[s, l : l + 1] * u[l]
            s_ref[s, rows] = total
            if 1 <= s <= 4:
                v = jnp.dot(mix_ref[ib], g_ref[s - 1], preferred_element_type=f32).reshape(NF, IB, CELLS)
                total = b_ref[s, 0:1] * v[0] + nb_ref[s - 1, 0:1] * u[0]
                for l in range(1, NF):
                    total = total + b_ref[s, l : l + 1] * v[l] + nb_ref[s - 1, l : l + 1] * u[l]
                t_ref[s - 1, rows] = total
        return 0

    lax.fori_loop(0, NIB, block, 0)
    for x in range(4):
        own = s_ref[x + 1]
        high = own.astype(bf16)
        low = (own - high.astype(f32)).astype(bf16)
        around = jnp.dot(high, near, preferred_element_type=f32) + jnp.dot(low, near, preferred_element_type=f32)
        out_ref[x] = (t_ref[x] - around - s_ref[x] - s_ref[x + 2]).astype(bf16)


def fill_faces(c0_ref, w_ref, inv_ref):
    place = iota((32, CELLS), 1)
    z_place = place & (NZ - 1)
    c = c0_ref[1]
    w_ref[0] = 0.5 * (c + c0_ref[2])
    w_ref[1] = 0.5 * (c + c0_ref[0])
    diag = w_ref[0] + w_ref[1]
    tests = ((CELLS - NZ, place < CELLS - NZ), (NZ, place >= NZ), (CELLS - 1, z_place < NZ - 1), (1, z_place > 0))
    for f, (amount, inside) in enumerate(tests):
        w = 0.5 * (c + jnp.where(inside, pltpu.roll(c, amount, 1), 0.0))
        diag = diag + w
        w_ref[2 + f] = jnp.where(inside, w, 0.0)
    inv_ref[...] = 1.0 / diag


def residual_kernel(img_ref, src_ref, c0_ref, res_ref, edge_ref, w_ref, inv_ref):
    fill_faces(c0_ref, w_ref, inv_ref)
    swap = swap_matrix(16, 32)
    for g in range(2):
        block = img_ref[:, 16 * g : 16 * (g + 1), :].reshape(512, CELLS)
        turned = jnp.dot(swap, block, preferred_element_type=f32).reshape(16, 32, CELLS)
        res_ref[16 * g : 16 * (g + 1)] = src_ref[16 * g : 16 * (g + 1)] - turned
    first_inv = inv_ref[...] * (1.0 / cheb_center)
    edge_ref[0] = res_ref[:, 0, :] * first_inv[0:1]
    edge_ref[1] = res_ref[:, 31, :] * first_inv[31:32]


def update_kernel(it_ref, res_ref, c0_ref, halo_ref, out_ref, w_ref, inv_ref):
    fill_faces(c0_ref, w_ref, inv_ref)
    row = iota((32, CELLS), 0)

    def one(mode, _):
        res = res_ref[mode]
        inv = inv_ref[...]
        first = res * inv * (1.0 / cheb_center)
        above = jnp.where(row == 31, halo_ref[1, pl.ds(mode, 1), :], pltpu.roll(first, 31, 0))
        below = jnp.where(row == 0, halo_ref[0, pl.ds(mode, 1), :], pltpu.roll(first, 1, 0))
        around = w_ref[0] * above + w_ref[1] * below
        for f, amount in enumerate((CELLS - NZ, NZ, CELLS - 1, 1)):
            around = around + w_ref[2 + f] * pltpu.roll(first, amount, 1)
        smoothed = res * (1.0 - 1.0 / cheb_center) + around
        second = rho_one * rho_zero * first + (2.0 * rho_one / cheb_radius) * smoothed * inv
        out_ref[mode] = it_ref[mode] + first + second
        return 0

    lax.fori_loop(0, 32, one, 0)


VM = pl.BlockSpec(memory_space=pltpu.VMEM)


def call(kernel, outs, ins, scratch):
    return pl.pallas_call(
        kernel,
        out_shape=outs,
        in_specs=[VM] * ins,
        out_specs=jax.tree.map(lambda _: VM, outs),
        scratch_shapes=scratch,
        compiler_params=pltpu.CompilerParams(vmem_limit_bytes=60 * 2**20),
    )


def swap_edges(low_side, high_side, axis):
    count = lax.axis_size(axis)
    forward = [(i, i + 1) for i in range(count - 1)]
    backward = [(b, a) for a, b in forward]
    return lax.ppermute(high_side, axis, forward), lax.ppermute(low_side, axis, backward)


def body(iterate, source, mean_coef, kl_fields, tri_index, tri_value):
    sds = jax.ShapeDtypeStruct
    mix, rows = call(
        prepare_kernel,
        (sds((NIB, NF * IB, P_SIZE), bf16), sds((32, 32, CELLS), bf16)),
        3,
        [pltpu.VMEM((P_SIZE, 64), f32)],
    )(tri_index.T, tri_value[None], iterate)
    coef = jnp.concatenate([mean_coef[None], kl_fields], 0)
    low, high = swap_edges(coef[:, :1], coef[:, -1:], "dom")
    coef = jnp.concatenate([low, coef, high], 1)
    c0 = jnp.stack([coef[0, 0:32], coef[0, 1:33], coef[0, 2:34]])
    low, high = swap_edges(rows[:1], rows[-1:], "dom")
    rows = jnp.concatenate([low, rows, high], 0)
    group = lax.axis_index("mode")
    mine = 0.5 * lax.dynamic_slice_in_dim(coef, group * 4, 6, 1)
    beta = jnp.pad(jnp.swapaxes(mine, 0, 1), ((0, 0), (0, 24 - NF), (0, 0)))
    windows = jnp.stack([rows[4 * d : 4 * d + 6] for d in range(8)])
    got = lax.all_to_all(windows, "mode", 0, 0, tiled=True)
    panel = jnp.swapaxes(got, 0, 1).reshape(6, P_SIZE, CELLS)
    image = call(
        image_kernel,
        sds((4, P_SIZE, CELLS), bf16),
        3,
        [
            pltpu.VMEM((4, P_SIZE, CELLS), bf16),
            pltpu.VMEM((4, 24, CELLS), f32),
            pltpu.VMEM((6, P_SIZE, CELLS), f32),
            pltpu.VMEM((4, P_SIZE, CELLS), f32),
        ],
    )(panel, mix, beta)
    back = jnp.swapaxes(image.reshape(4, 8, 32, CELLS), 0, 1)
    back = lax.all_to_all(back, "mode", 0, 0, tiled=True).reshape(32, 32, CELLS)
    faces = [pltpu.VMEM((6, 32, CELLS), f32), pltpu.VMEM((32, CELLS), f32)]
    block = sds((32, 32, CELLS), f32)
    residual, edges = call(residual_kernel, (block, sds((2, 32, CELLS), f32)), 3, faces)(back, source, c0)
    low, high = swap_edges(edges[0], edges[1], "dom")
    updated = call(update_kernel, block, 4, faces)(iterate, residual, c0, jnp.stack([low, high]))
    return updated, residual


def solution(mesh):
    return jax.shard_map(
        body,
        mesh=mesh,
        in_specs=(
            P("mode", "dom", None),
            P("mode", "dom", None),
            P("dom", None),
            P(None, "dom", None),
            P(),
            P(),
        ),
        out_specs=(P("mode", "dom", None), P("mode", "dom", None)),
        check_vma=False,
    )
```

```python
import jax
import jax.numpy as jnp
from jax import lax
from jax.experimental import pallas as pl
from jax.experimental.pallas import tpu as pltpu
from jax.sharding import PartitionSpec as P

P_SIZE = 256
NF = 21
NZ = 16
CELLS = 256
IB = 32
NIB = P_SIZE // IB
ENTRIES = P_SIZE * NF

cheb_center = 1.125
cheb_radius = 0.875
sigma = cheb_center / cheb_radius
rho_zero = 1.0 / sigma
rho_one = 1.0 / (2.0 * sigma - rho_zero)

f32 = jnp.float32
bf16 = jnp.bfloat16
i32 = jnp.int32


def iota(shape, dim):
    return lax.broadcasted_iota(i32, shape, dim)


def plane_neighbours():
    q = iota((CELLS, CELLS), 0)
    p = iota((CELLS, CELLS), 1)
    far = jnp.abs(q - p)
    same = (q >> 4) == (p >> 4)
    return jnp.where((far == NZ) | ((far == 1) & same), 1.0, 0.0).astype(bf16)


def build_mixing(tri_ref, val_ref, mix_ref, table_ref):
    mode = iota((P_SIZE, 256), 0)
    level = iota((32, 256), 0)

    def gather(step, total):
        here = pl.ds(pl.multiple_of(step * 256, 256), 256)
        worth = jnp.concatenate([val_ref[pl.ds(2 * step, 1)], val_ref[pl.ds(2 * step + 1, 1)]], 1)
        hot = jnp.where(mode == tri_ref[0:1, here], 1.0, 0.0).astype(bf16)
        mine = level == tri_ref[2:3, here]
        coef = jnp.where(mine, worth, 0.0).astype(bf16)
        trial = jnp.where(mine, tri_ref[1:2, here].astype(f32), 0.0).astype(bf16)
        both = jnp.concatenate([coef, trial], 0)
        return total + lax.dot_general(
            hot, both, (((1,), (1,)), ((), ())), preferred_element_type=f32
        )

    table_ref[...] = lax.fori_loop(0, ENTRIES // 256, gather, jnp.zeros((P_SIZE, 64), f32))
    column = iota((P_SIZE, P_SIZE), 1).astype(f32)
    for l in range(NF):
        coef = table_ref[:, l : l + 1]
        trial = table_ref[:, 32 + l : 33 + l]
        panel = jnp.where(column == trial, coef, 0.0).astype(bf16)
        mix_ref[:, l * IB : (l + 1) * IB, :] = panel.reshape(NIB, IB, P_SIZE)


def swap_matrix(major, minor):
    n = major * minor
    r = iota((n, n), 0)
    c = iota((n, n), 1)
    shift = minor.bit_length() - 1
    wanted = (r & (minor - 1)) * major + (r >> shift)
    return jnp.where(c == wanted, 1.0, 0.0).astype(bf16)


def lane_neighbours(x, z_place, place):
    up = jnp.where(z_place < NZ - 1, pltpu.roll(x, CELLS - 1, x.ndim - 1), 0.0)
    down = jnp.where(z_place > 0, pltpu.roll(x, 1, x.ndim - 1), 0.0)
    far = jnp.where(place < CELLS - NZ, pltpu.roll(x, CELLS - NZ, x.ndim - 1), 0.0)
    near = jnp.where(place >= NZ, pltpu.roll(x, NZ, x.ndim - 1), 0.0)
    return up + down + far + near


def fill_faces(c0_ref, w_ref, inv_ref):
    place = iota((32, CELLS), 1)
    z_place = place & (NZ - 1)
    c = c0_ref[1]
    w_ref[0] = 0.5 * (c + c0_ref[2])
    w_ref[1] = 0.5 * (c + c0_ref[0])
    diag = w_ref[0] + w_ref[1]
    tests = ((CELLS - NZ, place < CELLS - NZ), (NZ, place >= NZ), (CELLS - 1, z_place < NZ - 1), (1, z_place > 0))
    for f, (amount, inside) in enumerate(tests):
        w = 0.5 * (c + jnp.where(inside, pltpu.roll(c, amount, 1), 0.0))
        diag = diag + w
        w_ref[2 + f] = jnp.where(inside, w, 0.0)
    inv_ref[...] = 1.0 / diag


MESH = pl.DeviceIdType.MESH
GROUP = 8


def row_of(device, k):
    core = lax.rem(device, 2)
    return 8 * (device // 2) + core * (3 + k) + (1 - core) * (4 - k)


def fused_kernel(
    it_hbm, src_hbm, mean_ref, kl_hbm, tri_ref, val_ref, upd_ref, res_ref,
    it_ref, src_ref, kl_ref, rows_ref, edge_ref, r_ref, mix_ref, table_ref, g_ref, b_ref, nb_ref, s_ref, t_ref,
    ce_ref, ch_ref, out_ref, img_ref, fe_ref, fh_ref, c0_ref, w_ref, inv_ref,
    local_sem, edge_sem, send_sem, recv_sem, coef_sem, back_sem, home_sem, first_sem,
):
    d = lax.axis_index("dom")
    m = lax.axis_index("mode")
    count = lax.axis_size("dom")
    up = lax.rem(d + 1, count)
    down = lax.rem(d + count - 1, count)
    sibling = m + 1 - 2 * lax.rem(m, 2)
    peers = [lax.rem(m + p, GROUP) for p in range(1, GROUP)]
    own_modes = pl.ds(pl.multiple_of(m * 32, 32), 32)

    def send(source, target, device, sent, got):
        copy = pltpu.make_async_remote_copy(
            src_ref=source, dst_ref=target, send_sem=sent, recv_sem=got, device_id=device, device_id_type=MESH
        )
        copy.start()
        return copy

    def drain(ref, sem):
        pltpu.make_async_copy(ref, ref, sem).wait()

    loads = [
        pltpu.make_async_copy(a, b, local_sem.at[i])
        for i, (a, b) in enumerate(((it_hbm, it_ref), (kl_hbm, kl_ref), (src_hbm, src_ref)))
    ]
    for load in loads:
        load.start()
    barrier = pltpu.get_barrier_semaphore()
    for peer in peers:
        pl.semaphore_signal(barrier, inc=1, device_id=(d, peer), device_id_type=MESH)
    for other in (up, down):
        pl.semaphore_signal(barrier, inc=1, device_id=(other, m), device_id_type=MESH)

    loads[0].wait()
    swap = swap_matrix(32, 16)
    for g in range(2):
        block = it_ref[16 * g : 16 * (g + 1)].astype(bf16).reshape(512, CELLS)
        turned = jnp.dot(swap, block, preferred_element_type=f32).astype(bf16)
        rows_ref[:, 16 * g : 16 * (g + 1), :] = turned.reshape(32, 16, CELLS)
    loads[1].wait()
    blank = jnp.zeros((3, CELLS), f32)
    for side, row in ((0, 0), (1, 31)):
        ce_ref[side] = jnp.concatenate([mean_ref[row : row + 1], kl_ref[:, row, :], blank], 0)
    pl.semaphore_wait(barrier, GROUP + 1)

    edges = [
        send(rows_ref.at[31], edge_ref.at[0], (up, m), edge_sem.at[0], edge_sem.at[2]),
        send(rows_ref.at[0], edge_ref.at[1], (down, m), edge_sem.at[1], edge_sem.at[3]),
    ]
    coefs = [
        send(ce_ref.at[1], ch_ref.at[0], (up, m), coef_sem.at[0], coef_sem.at[2]),
        send(ce_ref.at[0], ch_ref.at[1], (down, m), coef_sem.at[1], coef_sem.at[3]),
    ]
    for k in range(1, 6):
        for peer in peers:
            row = row_of(peer, k)

            def pass_row():
                send(rows_ref.at[row], r_ref.at[k, own_modes], (d, peer), send_sem.at[k], recv_sem.at[k])

            if k < 5:
                pass_row()
            else:
                pl.when((row >= 0) & (row < 32))(pass_row)
        row = row_of(m, k)

        def keep_row():
            pltpu.make_async_copy(rows_ref.at[row], r_ref.at[k, own_modes], recv_sem.at[k]).start()

        if k < 5:
            keep_row()
        else:
            pl.when((row >= 0) & (row < 32))(keep_row)

    build_mixing(tri_ref, val_ref, mix_ref, table_ref)

    for side, holder in ((0, 0), (1, GROUP - 1)):
        edges[side].wait_recv()

        @pl.when(m == holder)
        def _():
            pltpu.make_async_copy(edge_ref.at[side], r_ref.at[5, own_modes], recv_sem.at[5]).start()

        @pl.when(m != holder)
        def _():
            send(edge_ref.at[side], r_ref.at[5, own_modes], (d, holder), send_sem.at[5], recv_sem.at[5])

    for copy in coefs:
        copy.wait_recv()
    first_edge = jnp.where(d == 0, 0.0, 1.0)
    last_edge = jnp.where(d == count - 1, 0.0, 1.0)
    outer = jnp.where(m == 0, first_edge, jnp.where(m == GROUP - 1, last_edge, 1.0))
    b_ref[...] = jnp.zeros_like(b_ref)
    for k in range(6):
        row = row_of(m, k)
        if k == 5:
            row = jnp.minimum(jnp.maximum(row, 0), 31)
        mean_row = mean_ref[pl.ds(row, 1), :]
        kl_row = kl_ref[:, pl.ds(row, 1), :].reshape(NF - 1, CELLS)
        here = jnp.concatenate([mean_row, kl_row, blank], 0)
        if k == 5:
            here = jnp.where(m == 0, ch_ref[0], jnp.where(m == GROUP - 1, ch_ref[1], here)) * outer
        b_ref[k] = 0.5 * here
    place = iota((24, CELLS), 1)
    for k in range(1, 5):
        nb_ref[k - 1] = b_ref[k - 1] + b_ref[k + 1] + lane_neighbours(b_ref[k], place & (NZ - 1), place)

    row = iota((32, CELLS), 0)
    mean = mean_ref[...]
    c0_ref[0] = jnp.where(row == 0, ch_ref[0, 0:1] * first_edge, pltpu.roll(mean, 1, 0))
    c0_ref[1] = mean
    c0_ref[2] = jnp.where(row == 31, ch_ref[1, 0:1] * last_edge, pltpu.roll(mean, 31, 0))
    fill_faces(c0_ref, w_ref, inv_ref)
    near = plane_neighbours()

    def mix_slot(k):
        def block(ib, _):
            rows = pl.ds(pl.multiple_of(ib * IB, IB), IB)
            u = jnp.dot(mix_ref[ib], r_ref[k], preferred_element_type=f32).reshape(NF, IB, CELLS)
            total = b_ref[k, 0:1] * u[0]
            for l in range(1, NF):
                total = total + b_ref[k, l : l + 1] * u[l]
            s_ref[k, rows] = total
            if 1 <= k <= 4:
                total = nb_ref[k - 1, 0:1] * u[0]
                for l in range(1, NF):
                    total = total + nb_ref[k - 1, l : l + 1] * u[l]
                t_ref[k - 1, rows] = total
            return 0

        lax.fori_loop(0, NIB, block, 0)

    def finish_row(k):
        own = r_ref[k]
        ahead = r_ref[k + 1].astype(f32)
        if k == 4:
            ahead = ahead * outer
        around = jnp.dot(own, near, preferred_element_type=f32)
        g_ref[...] = (6.0 * own.astype(f32) - around - r_ref[k - 1].astype(f32) - ahead).astype(bf16)

        def block(ib, _):
            rows = pl.ds(pl.multiple_of(ib * IB, IB), IB)
            v = jnp.dot(mix_ref[ib], g_ref[...], preferred_element_type=f32).reshape(NF, IB, CELLS)
            total = t_ref[k - 1, rows]
            for l in range(NF):
                total = total + b_ref[k, l : l + 1] * v[l]
            t_ref[k - 1, rows] = total
            return 0

        lax.fori_loop(0, NIB, block, 0)
        own = s_ref[k]
        high = own.astype(bf16)
        low = (own - high.astype(f32)).astype(bf16)
        around = jnp.dot(high, near, preferred_element_type=f32) + jnp.dot(low, near, preferred_element_type=f32)
        out_ref[k - 1] = (t_ref[k - 1] - around - s_ref[k - 1] - s_ref[k + 1]).astype(bf16)
        row = row_of(m, k)
        for peer in peers:
            modes = pl.ds(pl.multiple_of(peer * 32, 32), 32)
            send(out_ref.at[k - 1, modes], img_ref.at[row], (d, peer), back_sem.at[k - 1], home_sem.at[k - 1])
        pltpu.make_async_copy(out_ref.at[k - 1, own_modes], img_ref.at[row], home_sem.at[k - 1]).start()

    drain(r_ref.at[1], recv_sem.at[1])
    forward = send(r_ref.at[1], r_ref.at[0], (d, sibling), send_sem.at[0], recv_sem.at[0])
    mix_slot(1)
    drain(r_ref.at[2], recv_sem.at[2])
    mix_slot(2)
    forward.wait_recv()
    mix_slot(0)
    finish_row(1)
    for k in range(2, 5):
        drain(r_ref.at[k + 1], recv_sem.at[k + 1])
        mix_slot(k + 1)
        finish_row(k)

    loads[2].wait()
    for k in range(4):
        drain(img_ref.at[0:8], home_sem.at[k])
    first_inv = inv_ref[...] * (1.0 / cheb_center)
    for side, row in ((0, 0), (1, 31)):
        fe_ref[side] = (src_ref[:, row, :] - img_ref[row].astype(f32)) * first_inv[row : row + 1]
    firsts = [
        send(fe_ref.at[1], fh_ref.at[0], (up, m), first_sem.at[0], first_sem.at[2]),
        send(fe_ref.at[0], fh_ref.at[1], (down, m), first_sem.at[1], first_sem.at[3]),
    ]
    swap = swap_matrix(16, 32)
    for g in range(2):
        block = img_ref[:, 16 * g : 16 * (g + 1), :].reshape(512, CELLS)
        turned = jnp.dot(swap, block, preferred_element_type=f32).reshape(16, 32, CELLS)
        res_ref[16 * g : 16 * (g + 1)] = src_ref[16 * g : 16 * (g + 1)] - turned
    for copy in firsts:
        copy.wait_recv()
    row = iota((32, CELLS), 0)

    def update(mode, _):
        res = res_ref[mode]
        inv = inv_ref[...]
        first = res * inv * (1.0 / cheb_center)
        above = jnp.where(row == 31, fh_ref[1, pl.ds(mode, 1), :] * last_edge, pltpu.roll(first, 31, 0))
        below = jnp.where(row == 0, fh_ref[0, pl.ds(mode, 1), :] * first_edge, pltpu.roll(first, 1, 0))
        around = w_ref[0] * above + w_ref[1] * below
        for f, amount in enumerate((CELLS - NZ, NZ, CELLS - 1, 1)):
            around = around + w_ref[2 + f] * pltpu.roll(first, amount, 1)
        smoothed = res * (1.0 - 1.0 / cheb_center) + around
        second = rho_one * rho_zero * first + (2.0 * rho_one / cheb_radius) * smoothed * inv
        upd_ref[mode] = it_ref[mode] + first + second
        return 0

    lax.fori_loop(0, 32, update, 0)

    for copy in edges + coefs + firsts + [forward]:
        copy.wait_send()
    sent = pl.ds(0, 32 * (GROUP - 1))
    for k in range(1, 6):
        drain(r_ref.at[k, sent], send_sem.at[k])
    for k in range(4):
        drain(out_ref.at[k, sent], back_sem.at[k])


def body(iterate, source, mean_coef, kl_fields, tri_index, tri_value):
    sds = jax.ShapeDtypeStruct
    vm = pl.BlockSpec(memory_space=pltpu.VMEM)
    anywhere = pl.BlockSpec(memory_space=pl.ANY)
    block = sds((32, 32, CELLS), f32)
    dma = pltpu.SemaphoreType.DMA
    return pl.pallas_call(
        fused_kernel,
        out_shape=(block, block),
        in_specs=[anywhere, anywhere, vm, anywhere, vm, vm],
        out_specs=(vm, vm),
        scratch_shapes=[
            pltpu.VMEM((32, 32, CELLS), f32),
            pltpu.VMEM((32, 32, CELLS), f32),
            pltpu.VMEM((NF - 1, 32, CELLS), f32),
            pltpu.VMEM((32, 32, CELLS), bf16),
            pltpu.VMEM((2, 32, CELLS), bf16),
            pltpu.VMEM((6, P_SIZE, CELLS), bf16),
            pltpu.VMEM((NIB, NF * IB, P_SIZE), bf16),
            pltpu.VMEM((P_SIZE, 64), f32),
            pltpu.VMEM((P_SIZE, CELLS), bf16),
            pltpu.VMEM((6, 24, CELLS), f32),
            pltpu.VMEM((4, 24, CELLS), f32),
            pltpu.VMEM((6, P_SIZE, CELLS), f32),
            pltpu.VMEM((4, P_SIZE, CELLS), f32),
            pltpu.VMEM((2, 24, CELLS), f32),
            pltpu.VMEM((2, 24, CELLS), f32),
            pltpu.VMEM((4, P_SIZE, CELLS), bf16),
            pltpu.VMEM((32, 32, CELLS), bf16),
            pltpu.VMEM((2, 32, CELLS), f32),
            pltpu.VMEM((2, 32, CELLS), f32),
            pltpu.VMEM((3, 32, CELLS), f32),
            pltpu.VMEM((6, 32, CELLS), f32),
            pltpu.VMEM((32, CELLS), f32),
            dma((3,)),
            dma((4,)),
            dma((6,)),
            dma((6,)),
            dma((4,)),
            dma((4,)),
            dma((4,)),
            dma((4,)),
        ],
        compiler_params=pltpu.CompilerParams(
            collective_id=0, has_side_effects=True, vmem_limit_bytes=60 * 2**20
        ),
    )(iterate, source, mean_coef, kl_fields, tri_index.T, tri_value.reshape(42, 128))


def solution(mesh):
    return jax.shard_map(
        body,
        mesh=mesh,
        in_specs=(
            P("mode", "dom", None),
            P("mode", "dom", None),
            P("dom", None),
            P(None, "dom", None),
            P(),
            P(),
        ),
        out_specs=(P("mode", "dom", None), P("mode", "dom", None)),
        check_vma=False,
    )
```

```python
import jax
import jax.numpy as jnp
from jax import lax
from jax.experimental import pallas as pl
from jax.experimental.pallas import tpu as pltpu
from jax.sharding import PartitionSpec as P

P_SIZE = 256
NF = 21
NZ = 16
CELLS = 256
IB = 32
NIB = P_SIZE // IB
ENTRIES = P_SIZE * NF

cheb_center = 1.125
cheb_radius = 0.875
sigma = cheb_center / cheb_radius
rho_zero = 1.0 / sigma
rho_one = 1.0 / (2.0 * sigma - rho_zero)

f32 = jnp.float32
bf16 = jnp.bfloat16
i32 = jnp.int32


def iota(shape, dim):
    return lax.broadcasted_iota(i32, shape, dim)


def plane_neighbours():
    q = iota((CELLS, CELLS), 0)
    p = iota((CELLS, CELLS), 1)
    far = jnp.abs(q - p)
    same = (q >> 4) == (p >> 4)
    return jnp.where((far == NZ) | ((far == 1) & same), 1.0, 0.0).astype(bf16)


def fill_table(tri_ref, val_ref, table_ref):
    mode = iota((P_SIZE, 256), 0)
    level = iota((32, 256), 0)

    def gather(step, total):
        here = pl.ds(pl.multiple_of(step * 256, 256), 256)
        worth = jnp.concatenate([val_ref[pl.ds(2 * step, 1)], val_ref[pl.ds(2 * step + 1, 1)]], 1)
        hot = jnp.where(mode == tri_ref[0:1, here], 1.0, 0.0).astype(bf16)
        mine = level == tri_ref[2:3, here]
        coef = jnp.where(mine, worth, 0.0).astype(bf16)
        trial = jnp.where(mine, tri_ref[1:2, here].astype(f32), 0.0).astype(bf16)
        both = jnp.concatenate([coef, trial], 0)
        return total + lax.dot_general(
            hot, both, (((1,), (1,)), ((), ())), preferred_element_type=f32
        )

    table_ref[...] = lax.fori_loop(0, ENTRIES // 256, gather, jnp.zeros((P_SIZE, 64), f32))


def fill_mixing(table_ref, mix_ref):
    column = iota((P_SIZE, P_SIZE), 1).astype(f32)
    for l in range(NF):
        coef = table_ref[:, l : l + 1]
        trial = table_ref[:, 32 + l : 33 + l]
        panel = jnp.where(column == trial, coef, 0.0).astype(bf16)
        mix_ref[:, l * IB : (l + 1) * IB, :] = panel.reshape(NIB, IB, P_SIZE)


def swap_matrix(major, minor):
    n = major * minor
    r = iota((n, n), 0)
    c = iota((n, n), 1)
    shift = minor.bit_length() - 1
    wanted = (r & (minor - 1)) * major + (r >> shift)
    return jnp.where(c == wanted, 1.0, 0.0).astype(bf16)


def lane_neighbours(x, z_place, place):
    up = jnp.where(z_place < NZ - 1, pltpu.roll(x, CELLS - 1, x.ndim - 1), 0.0)
    down = jnp.where(z_place > 0, pltpu.roll(x, 1, x.ndim - 1), 0.0)
    far = jnp.where(place < CELLS - NZ, pltpu.roll(x, CELLS - NZ, x.ndim - 1), 0.0)
    near = jnp.where(place >= NZ, pltpu.roll(x, NZ, x.ndim - 1), 0.0)
    return up + down + far + near


def fill_faces(c0_ref, w_ref, inv_ref):
    place = iota((32, CELLS), 1)
    z_place = place & (NZ - 1)
    c = c0_ref[1]
    w_ref[0] = 0.5 * (c + c0_ref[2])
    w_ref[1] = 0.5 * (c + c0_ref[0])
    diag = w_ref[0] + w_ref[1]
    tests = ((CELLS - NZ, place < CELLS - NZ), (NZ, place >= NZ), (CELLS - 1, z_place < NZ - 1), (1, z_place > 0))
    for f, (amount, inside) in enumerate(tests):
        w = 0.5 * (c + jnp.where(inside, pltpu.roll(c, amount, 1), 0.0))
        diag = diag + w
        w_ref[2 + f] = jnp.where(inside, w, 0.0)
    inv_ref[...] = 1.0 / diag


MESH = pl.DeviceIdType.MESH
GROUP = 8


def row_of(device, k):
    core = lax.rem(device, 2)
    return 8 * (device // 2) + core * (8 - k) + (1 - core) * (k - 1)


def exchange_kernel(
    it_hbm, src_hbm, mean_hbm, kl_hbm, tri_hbm, val_hbm, nat_ref, halo_ref, w_ref, inv_ref,
    it_ref, src_ref, mean_ref, kl_ref, tri_ref, val_ref, rows_ref, edge_ref, r_ref, mix_ref, table_ref, g_ref, b_ref, nb_ref, s_ref, t_ref,
    ce_ref, ch_ref, out_ref, img_ref, fe_ref, fh_ref, c0_ref,
    local_sem, edge_sem, send_sem, recv_sem, coef_sem, back_sem, home_sem, first_sem,
):
    d = lax.axis_index("dom")
    m = lax.axis_index("mode")
    count = lax.axis_size("dom")
    up = lax.rem(d + 1, count)
    down = lax.rem(d + count - 1, count)
    sibling = m + 1 - 2 * lax.rem(m, 2)
    peers = [lax.rem(m + p, GROUP) for p in range(1, GROUP)]
    own_modes = pl.ds(pl.multiple_of(m * 32, 32), 32)

    def send(source, target, device, sent, got):
        copy = pltpu.make_async_remote_copy(
            src_ref=source, dst_ref=target, send_sem=sent, recv_sem=got, device_id=device, device_id_type=MESH
        )
        copy.start()
        return copy

    def drain(ref, sem):
        pltpu.make_async_copy(ref, ref, sem).wait()

    loads = [
        pltpu.make_async_copy(a, b, local_sem.at[i])
        for i, (a, b) in enumerate(
            (
                (it_hbm, it_ref),
                (kl_hbm, kl_ref),
                (mean_hbm, mean_ref),
                (tri_hbm, tri_ref),
                (val_hbm, val_ref),
                (src_hbm, src_ref),
            )
        )
    ]
    for load in loads:
        load.start()
    barrier = pltpu.get_barrier_semaphore()
    for peer in peers:
        pl.semaphore_signal(barrier, inc=1, device_id=(d, peer), device_id_type=MESH)
    for other in (up, down):
        pl.semaphore_signal(barrier, inc=1, device_id=(other, m), device_id_type=MESH)

    loads[0].wait()
    swap = swap_matrix(32, 16)
    for g in range(2):
        block = it_ref[16 * g : 16 * (g + 1)].astype(bf16).reshape(512, CELLS)
        turned = jnp.dot(swap, block, preferred_element_type=f32).astype(bf16)
        rows_ref[:, 16 * g : 16 * (g + 1), :] = turned.reshape(32, 16, CELLS)
    loads[1].wait()
    loads[2].wait()
    blank = jnp.zeros((3, CELLS), f32)
    for side, row in ((0, 0), (1, 31)):
        ce_ref[side] = jnp.concatenate([mean_ref[row : row + 1], kl_ref[:, row, :], blank], 0)
    pl.semaphore_wait(barrier, GROUP + 1)

    def issue(k):
        for peer in peers:
            row = row_of(peer, k)

            def pass_row():
                send(rows_ref.at[row], r_ref.at[k, own_modes], (d, peer), send_sem.at[k], recv_sem.at[k])

            if k > 0:
                pass_row()
            else:
                pl.when((row >= 0) & (row < 32))(pass_row)
        row = row_of(m, k)

        def keep_row():
            pltpu.make_async_copy(rows_ref.at[row], r_ref.at[k, own_modes], recv_sem.at[k]).start()

        if k > 0:
            keep_row()
        else:
            pl.when((row >= 0) & (row < 32))(keep_row)

    def sent(k):
        drain(r_ref.at[k, pl.ds(0, 32 * (GROUP - 1))], send_sem.at[k])

    edges = [
        send(rows_ref.at[31], edge_ref.at[0], (up, m), edge_sem.at[0], edge_sem.at[2]),
        send(rows_ref.at[0], edge_ref.at[1], (down, m), edge_sem.at[1], edge_sem.at[3]),
    ]
    coefs = [
        send(ce_ref.at[1], ch_ref.at[0], (up, m), coef_sem.at[0], coef_sem.at[2]),
        send(ce_ref.at[0], ch_ref.at[1], (down, m), coef_sem.at[1], coef_sem.at[3]),
    ]
    issue(1)
    issue(0)
    loads[3].wait()
    loads[4].wait()
    fill_table(tri_ref, val_ref, table_ref)
    sent(1)
    issue(2)

    for side, holder in ((0, 0), (1, GROUP - 1)):
        edges[side].wait_recv()

        @pl.when(m == holder)
        def _():
            pltpu.make_async_copy(edge_ref.at[side], r_ref.at[0, own_modes], recv_sem.at[0]).start()

        @pl.when(m != holder)
        def _():
            send(edge_ref.at[side], r_ref.at[0, own_modes], (d, holder), send_sem.at[0], recv_sem.at[0])

    fill_mixing(table_ref, mix_ref)
    sent(0)
    issue(3)

    for copy in coefs:
        copy.wait_recv()
    first_edge = jnp.where(d == 0, 0.0, 1.0)
    last_edge = jnp.where(d == count - 1, 0.0, 1.0)
    outer = jnp.where(m == 0, first_edge, jnp.where(m == GROUP - 1, last_edge, 1.0))
    for k in range(6):
        row = row_of(m, k)
        if k == 0:
            row = jnp.minimum(jnp.maximum(row, 0), 31)
        mean_row = mean_ref[pl.ds(row, 1), :]
        kl_row = kl_ref[:, pl.ds(row, 1), :].reshape(NF - 1, CELLS)
        here = jnp.concatenate([mean_row, kl_row, blank], 0)
        if k == 0:
            here = jnp.where(m == 0, ch_ref[0], jnp.where(m == GROUP - 1, ch_ref[1], here)) * outer
        b_ref[k] = 0.5 * here
    place = iota((24, CELLS), 1)
    for k in range(1, 5):
        nb_ref[k - 1] = b_ref[k - 1] + b_ref[k + 1] + lane_neighbours(b_ref[k], place & (NZ - 1), place)

    row = iota((32, CELLS), 0)
    mean = mean_ref[...]
    c0_ref[0] = jnp.where(row == 0, ch_ref[0, 0:1] * first_edge, pltpu.roll(mean, 1, 0))
    c0_ref[1] = mean
    c0_ref[2] = jnp.where(row == 31, ch_ref[1, 0:1] * last_edge, pltpu.roll(mean, 31, 0))
    fill_faces(c0_ref, w_ref, inv_ref)
    near = plane_neighbours()

    def weigh(coef, u, total=None):
        for l in range(NF):
            term = coef[l : l + 1] * u[l]
            total = term if total is None else total + term
        return total

    def mixed(ib, panel):
        return jnp.dot(mix_ref[ib], panel, preferred_element_type=f32).reshape(NF, IB, CELLS)

    def take_plane(k):
        own = s_ref[k]
        high = own.astype(bf16)
        low = (own - high.astype(f32)).astype(bf16)
        around = jnp.dot(high, near, preferred_element_type=f32) + jnp.dot(low, near, preferred_element_type=f32)
        t_ref[k - 1] = t_ref[k - 1] - around

    def mix_slot(k):
        def block(ib, _):
            rows = pl.ds(pl.multiple_of(ib * IB, IB), IB)
            u = mixed(ib, r_ref[k])
            s_ref[k, rows] = weigh(b_ref[k], u)
            if k > 0:
                t_ref[k - 1, rows] = weigh(nb_ref[k - 1], u)
            return 0

        lax.fori_loop(0, NIB, block, 0)
        if k > 0:
            take_plane(k)

    def fill_differences(k):
        own = r_ref[k]
        behind = r_ref[k - 1].astype(f32)
        if k == 1:
            behind = behind * outer
        around = jnp.dot(own, near, preferred_element_type=f32)
        g_ref[...] = (6.0 * own.astype(f32) - around - behind - r_ref[k + 1].astype(f32)).astype(bf16)

    def finish_row(k):
        row = row_of(m, k)

        def block(i, _):
            ib = lax.rem(m + 1 + i, GROUP)
            before = lax.rem(m + i, GROUP)

            @pl.when(i > 0)
            def _():
                modes = pl.ds(pl.multiple_of(before * IB, IB), IB)
                send(out_ref.at[k - 1, modes], img_ref.at[row], (d, before), back_sem.at[k - 1], home_sem.at[k - 1])

            rows = pl.ds(pl.multiple_of(ib * IB, IB), IB)
            u = mixed(ib, r_ref[k + 1])
            following = weigh(b_ref[k + 1], u)
            s_ref[k + 1, rows] = following
            if k < 4:
                t_ref[k, rows] = weigh(nb_ref[k], u)
            v = mixed(ib, g_ref[...])
            total = weigh(b_ref[k], v, t_ref[k - 1, rows] - s_ref[k - 1, rows] - following).astype(bf16)
            out_ref[k - 1, rows] = total

            @pl.when(i == GROUP - 1)
            def _():
                img_ref[row] = total

            return 0

        lax.fori_loop(0, GROUP, block, 0)
        if k < 4:
            take_plane(k + 1)

    seven = pl.ds(0, GROUP - 1)
    drain(r_ref.at[1], recv_sem.at[1])
    mix_slot(1)
    drain(r_ref.at[0], recv_sem.at[0])
    mix_slot(0)
    sent(2)
    issue(4)
    drain(r_ref.at[2], recv_sem.at[2])
    fill_differences(1)
    finish_row(1)
    drain(r_ref.at[3], recv_sem.at[3])
    fill_differences(2)
    finish_row(2)
    drain(r_ref.at[4], recv_sem.at[4])
    forward = send(r_ref.at[4], r_ref.at[5], (d, sibling), send_sem.at[5], recv_sem.at[5])
    fill_differences(3)
    finish_row(3)
    loads[5].wait()
    drain(img_ref.at[seven], home_sem.at[0])
    first_inv = inv_ref[...] * (1.0 / cheb_center)
    for side, row in ((0, 0), (1, 31)):
        fe_ref[side] = (src_ref[:, row, :] - img_ref[row].astype(f32)) * first_inv[row : row + 1]
    forward.wait_recv()
    fill_differences(4)
    firsts = [
        send(fe_ref.at[1], fh_ref.at[0], (up, m), first_sem.at[0], first_sem.at[2]),
        send(fe_ref.at[0], fh_ref.at[1], (down, m), first_sem.at[1], first_sem.at[3]),
    ]
    finish_row(4)

    for copy in firsts:
        copy.wait_recv()
    halo_ref[0] = fh_ref[0] * first_edge
    halo_ref[1] = fh_ref[1] * last_edge
    for copy in edges + coefs + firsts + [forward]:
        copy.wait_send()
    for k in (3, 4):
        sent(k)
    for k in range(1, 4):
        drain(img_ref.at[seven], home_sem.at[k])
    swap = swap_matrix(16, 32)
    for g in range(2):
        block = img_ref[:, 16 * g : 16 * (g + 1), :].reshape(512, CELLS)
        turned = jnp.dot(swap, block, preferred_element_type=f32).astype(bf16)
        nat_ref[16 * g : 16 * (g + 1)] = turned.reshape(16, 32, CELLS)
    for k in range(4):
        drain(out_ref.at[k, pl.ds(0, 32 * (GROUP - 1))], back_sem.at[k])


STEP = 8


def correct_kernel(it_ref, src_ref, nat_ref, halo_ref, w_ref, inv_ref, upd_ref, res_ref):
    row = iota((32, CELLS), 0)

    def update(mode, _):
        res = src_ref[mode] - nat_ref[mode].astype(f32)
        res_ref[mode] = res
        inv = inv_ref[...]
        first = res * inv * (1.0 / cheb_center)
        above = jnp.where(row == 31, halo_ref[1, pl.ds(mode, 1), :], pltpu.roll(first, 31, 0))
        below = jnp.where(row == 0, halo_ref[0, pl.ds(mode, 1), :], pltpu.roll(first, 1, 0))
        around = w_ref[0] * above + w_ref[1] * below
        for f, amount in enumerate((CELLS - NZ, NZ, CELLS - 1, 1)):
            around = around + w_ref[2 + f] * pltpu.roll(first, amount, 1)
        smoothed = res * (1.0 - 1.0 / cheb_center) + around
        second = rho_one * rho_zero * first + (2.0 * rho_one / cheb_radius) * smoothed * inv
        upd_ref[mode] = it_ref[mode] + first + second
        return 0

    lax.fori_loop(0, STEP, update, 0, unroll=2)


def body(iterate, source, mean_coef, kl_fields, tri_index, tri_value):
    sds = jax.ShapeDtypeStruct
    vm = pl.BlockSpec(memory_space=pltpu.VMEM)
    hbm = pl.BlockSpec(memory_space=pltpu.HBM)
    dma = pltpu.SemaphoreType.DMA
    natural, halo, w, inv = pl.pallas_call(
        exchange_kernel,
        out_shape=(
            sds((32, 32, CELLS), bf16),
            sds((2, 32, CELLS), f32),
            sds((6, 32, CELLS), f32),
            sds((32, CELLS), f32),
        ),
        in_specs=[hbm] * 6,
        out_specs=(vm, vm, vm, vm),
        scratch_shapes=[
            pltpu.VMEM((32, 32, CELLS), f32),
            pltpu.VMEM((32, 32, CELLS), f32),
            pltpu.VMEM((32, CELLS), f32),
            pltpu.VMEM((NF - 1, 32, CELLS), f32),
            pltpu.VMEM((3, ENTRIES), i32),
            pltpu.VMEM((42, 128), f32),
            pltpu.VMEM((32, 32, CELLS), bf16),
            pltpu.VMEM((2, 32, CELLS), bf16),
            pltpu.VMEM((6, P_SIZE, CELLS), bf16),
            pltpu.VMEM((NIB, NF * IB, P_SIZE), bf16),
            pltpu.VMEM((P_SIZE, 64), f32),
            pltpu.VMEM((P_SIZE, CELLS), bf16),
            pltpu.VMEM((6, 24, CELLS), f32),
            pltpu.VMEM((4, 24, CELLS), f32),
            pltpu.VMEM((6, P_SIZE, CELLS), f32),
            pltpu.VMEM((4, P_SIZE, CELLS), f32),
            pltpu.VMEM((2, 24, CELLS), f32),
            pltpu.VMEM((2, 24, CELLS), f32),
            pltpu.VMEM((4, P_SIZE, CELLS), bf16),
            pltpu.VMEM((32, 32, CELLS), bf16),
            pltpu.VMEM((2, 32, CELLS), f32),
            pltpu.VMEM((2, 32, CELLS), f32),
            pltpu.VMEM((3, 32, CELLS), f32),
            dma((6,)),
            dma((4,)),
            dma((6,)),
            dma((6,)),
            dma((4,)),
            dma((4,)),
            dma((4,)),
            dma((4,)),
        ],
        compiler_params=pltpu.CompilerParams(
            collective_id=0, has_side_effects=True, vmem_limit_bytes=50 * 2**20
        ),
    )(*[
        pltpu.with_memory_space_constraint(x, pltpu.HBM)
        for x in (iterate, source, mean_coef, kl_fields, tri_index.T, tri_value.reshape(42, 128))
    ])

    big = pl.BlockSpec((STEP, 32, CELLS), lambda g: (g, 0, 0))
    return pl.pallas_call(
        correct_kernel,
        out_shape=(sds((32, 32, CELLS), f32), sds((32, 32, CELLS), f32)),
        grid=(32 // STEP,),
        in_specs=[
            big,
            big,
            big,
            pl.BlockSpec((2, STEP, CELLS), lambda g: (0, g, 0)),
            pl.BlockSpec((6, 32, CELLS), lambda g: (0, 0, 0)),
            pl.BlockSpec((32, CELLS), lambda g: (0, 0)),
        ],
        out_specs=(big, big),
        compiler_params=pltpu.CompilerParams(vmem_limit_bytes=16 * 2**20),
    )(iterate, source, natural, halo, w, inv)


def solution(mesh):
    return jax.shard_map(
        body,
        mesh=mesh,
        in_specs=(
            P("mode", "dom", None),
            P("mode", "dom", None),
            P("dom", None),
            P(None, "dom", None),
            P(),
            P(),
        ),
        out_specs=(P("mode", "dom", None), P("mode", "dom", None)),
        check_vma=False,
    )
```

```python
import jax
import jax.numpy as jnp
from jax import lax
from jax.experimental import pallas as pl
from jax.experimental.pallas import tpu as pltpu
from jax.sharding import PartitionSpec as P

P_SIZE = 256
NF = 21
NZ = 16
CELLS = 256
IB = 32
NIB = P_SIZE // IB
ENTRIES = P_SIZE * NF

cheb_center = 1.125
cheb_radius = 0.875
sigma = cheb_center / cheb_radius
rho_zero = 1.0 / sigma
rho_one = 1.0 / (2.0 * sigma - rho_zero)

f32 = jnp.float32
bf16 = jnp.bfloat16
i32 = jnp.int32


def iota(shape, dim):
    return lax.broadcasted_iota(i32, shape, dim)


def plane_neighbours():
    q = iota((CELLS, CELLS), 0)
    p = iota((CELLS, CELLS), 1)
    far = jnp.abs(q - p)
    same = (q >> 4) == (p >> 4)
    return jnp.where((far == NZ) | ((far == 1) & same), 1.0, 0.0).astype(bf16)


def fill_table(tri_ref, val_ref, table_ref):
    mode = iota((P_SIZE, 256), 0)
    level = iota((32, 256), 0)

    def gather(step, total):
        here = pl.ds(pl.multiple_of(step * 256, 256), 256)
        worth = jnp.concatenate([val_ref[pl.ds(2 * step, 1)], val_ref[pl.ds(2 * step + 1, 1)]], 1)
        hot = jnp.where(mode == tri_ref[0:1, here], 1.0, 0.0).astype(bf16)
        mine = level == tri_ref[2:3, here]
        coef = jnp.where(mine, worth, 0.0).astype(bf16)
        trial = jnp.where(mine, tri_ref[1:2, here].astype(f32), 0.0).astype(bf16)
        both = jnp.concatenate([coef, trial], 0)
        return total + lax.dot_general(
            hot, both, (((1,), (1,)), ((), ())), preferred_element_type=f32
        )

    table_ref[...] = lax.fori_loop(0, ENTRIES // 256, gather, jnp.zeros((P_SIZE, 64), f32))


def fill_mixing(table_ref, mix_ref):
    column = iota((P_SIZE, P_SIZE), 1).astype(f32)
    for l in range(NF):
        coef = table_ref[:, l : l + 1]
        trial = table_ref[:, 32 + l : 33 + l]
        panel = jnp.where(column == trial, coef, 0.0).astype(bf16)
        mix_ref[:, l * IB : (l + 1) * IB, :] = panel.reshape(NIB, IB, P_SIZE)


def swap_matrix(major, minor):
    n = major * minor
    r = iota((n, n), 0)
    c = iota((n, n), 1)
    shift = minor.bit_length() - 1
    wanted = (r & (minor - 1)) * major + (r >> shift)
    return jnp.where(c == wanted, 1.0, 0.0).astype(bf16)


def lane_neighbours(x, z_place, place):
    up = jnp.where(z_place < NZ - 1, pltpu.roll(x, CELLS - 1, x.ndim - 1), 0.0)
    down = jnp.where(z_place > 0, pltpu.roll(x, 1, x.ndim - 1), 0.0)
    far = jnp.where(place < CELLS - NZ, pltpu.roll(x, CELLS - NZ, x.ndim - 1), 0.0)
    near = jnp.where(place >= NZ, pltpu.roll(x, NZ, x.ndim - 1), 0.0)
    return up + down + far + near


def fill_faces(c0_ref, w_ref, inv_ref):
    place = iota((32, CELLS), 1)
    z_place = place & (NZ - 1)
    c = c0_ref[1]
    w_ref[0] = 0.5 * (c + c0_ref[2])
    w_ref[1] = 0.5 * (c + c0_ref[0])
    diag = w_ref[0] + w_ref[1]
    tests = ((CELLS - NZ, place < CELLS - NZ), (NZ, place >= NZ), (CELLS - 1, z_place < NZ - 1), (1, z_place > 0))
    for f, (amount, inside) in enumerate(tests):
        w = 0.5 * (c + jnp.where(inside, pltpu.roll(c, amount, 1), 0.0))
        diag = diag + w
        w_ref[2 + f] = jnp.where(inside, w, 0.0)
    inv_ref[...] = 1.0 / diag


MESH = pl.DeviceIdType.MESH
GROUP = 8


def row_of(device, k):
    core = lax.rem(device, 2)
    return 8 * (device // 2) + core * (8 - k) + (1 - core) * (k - 1)


def exchange_kernel(
    it_hbm, src_hbm, mean_hbm, kl_hbm, tri_hbm, val_hbm, nat_ref, halo_ref, w_ref, inv_ref,
    it_ref, src_ref, mean_ref, kl_ref, tri_ref, val_ref, rows_ref, pair_ref, edge_ref, r_ref, mix_ref, table_ref, g_ref, b_ref, nb_ref, s_ref, t_ref,
    ce_ref, ch_ref, out_ref, img_ref, fe_ref, fh_ref, c0_ref,
    local_sem, edge_sem, send_sem, recv_sem, coef_sem, back_sem, home_sem, first_sem, pair_sem, go_sem,
):
    d = lax.axis_index("dom")
    m = lax.axis_index("mode")
    count = lax.axis_size("dom")
    up = lax.rem(d + 1, count)
    down = lax.rem(d + count - 1, count)
    sibling = m + 1 - 2 * lax.rem(m, 2)
    peers = [lax.rem(m + p, GROUP) for p in range(1, GROUP)]
    own_modes = pl.ds(pl.multiple_of(m * 32, 32), 32)

    def send(source, target, device, sent, got):
        copy = pltpu.make_async_remote_copy(
            src_ref=source, dst_ref=target, send_sem=sent, recv_sem=got, device_id=device, device_id_type=MESH
        )
        copy.start()
        return copy

    def drain(ref, sem):
        pltpu.make_async_copy(ref, ref, sem).wait()

    loads = [
        pltpu.make_async_copy(a, b, local_sem.at[i])
        for i, (a, b) in enumerate(
            (
                (it_hbm, it_ref),
                (kl_hbm, kl_ref),
                (mean_hbm, mean_ref),
                (tri_hbm, tri_ref),
                (val_hbm, val_ref),
                (src_hbm, src_ref),
            )
        )
    ]
    for load in loads:
        load.start()
    even = lax.rem(m, 2) == 0
    odd = lax.rem(m, 2) == 1
    barrier = pltpu.get_barrier_semaphore()
    for peer in peers:

        @pl.when(lax.rem(peer, 2) == 0)
        def _():
            pl.semaphore_signal(barrier, inc=1, device_id=(d, peer), device_id_type=MESH)

    @pl.when(odd)
    def _():
        for other in (up, down):
            pl.semaphore_signal(barrier, inc=1, device_id=(other, m), device_id_type=MESH)

    loads[0].wait()
    swap = swap_matrix(32, 16)
    for g in range(2):
        block = it_ref[16 * g : 16 * (g + 1)].astype(bf16).reshape(512, CELLS)
        turned = jnp.dot(swap, block, preferred_element_type=f32).astype(bf16)
        rows_ref[:, 16 * g : 16 * (g + 1), :] = turned.reshape(32, 16, CELLS)
    pair_ref[0, 32:64] = rows_ref[0]
    pair_ref[1, 32:64] = rows_ref[31]
    loads[1].wait()
    loads[2].wait()
    blank = jnp.zeros((3, CELLS), f32)
    for side, row in ((0, 0), (1, 31)):
        ce_ref[side] = jnp.concatenate([mean_ref[row : row + 1], kl_ref[:, row, :], blank], 0)

    @pl.when(even)
    def _():
        pl.semaphore_wait(barrier, GROUP - 1)
        pl.semaphore_signal(go_sem, inc=1, device_id=(d, sibling), device_id_type=MESH)

    @pl.when(odd)
    def _():
        pl.semaphore_wait(go_sem, 1)

    def issue(k):
        for peer in peers:
            row = row_of(peer, k)

            def pass_row():
                send(rows_ref.at[row], r_ref.at[k, own_modes], (d, peer), send_sem.at[k], recv_sem.at[k])

            if k > 0:
                pass_row()
            else:
                pl.when((row >= 0) & (row < 32))(pass_row)
        row = row_of(m, k)

        def keep_row():
            pltpu.make_async_copy(rows_ref.at[row], r_ref.at[k, own_modes], recv_sem.at[k]).start()

        if k > 0:
            keep_row()
        else:
            pl.when((row >= 0) & (row < 32))(keep_row)

    def sent(k):
        drain(r_ref.at[k, pl.ds(0, 32 * (GROUP - 1))], send_sem.at[k])

    @pl.when(even)
    def _():
        for side, row in ((0, 0), (1, 31)):
            send(rows_ref.at[row], pair_ref.at[side, pl.ds(0, 32)], (d, sibling), pair_sem.at[side], pair_sem.at[2 + side])

    issue(1)
    issue(2)
    loads[3].wait()
    loads[4].wait()
    fill_table(tri_ref, val_ref, table_ref)
    sent(1)
    issue(3)
    fill_mixing(table_ref, mix_ref)

    first_edge = jnp.where(d == 0, 0.0, 1.0)
    last_edge = jnp.where(d == count - 1, 0.0, 1.0)
    outer = jnp.where(m == 0, first_edge, jnp.where(m == GROUP - 1, last_edge, 1.0))

    def coef_row(row):
        kl_row = kl_ref[:, pl.ds(row, 1), :].reshape(NF - 1, CELLS)
        return jnp.concatenate([mean_ref[pl.ds(row, 1), :], kl_row, blank], 0)

    for k in range(1, 6):
        b_ref[k] = 0.5 * coef_row(row_of(m, k))
    place = iota((24, CELLS), 1)
    for k in range(1, 5):
        beside = b_ref[k + 1] if k == 1 else b_ref[k - 1] + b_ref[k + 1]
        nb_ref[k - 1] = beside + lane_neighbours(b_ref[k], place & (NZ - 1), place)
    near = plane_neighbours()
    sent(2)
    issue(4)

    def weigh(coef, u, total=None):
        for l in range(NF):
            term = coef[l : l + 1] * u[l]
            total = term if total is None else total + term
        return total

    def mixed(ib, panel):
        return jnp.dot(mix_ref[ib], panel, preferred_element_type=f32).reshape(NF, IB, CELLS)

    def take_plane(k):
        own = s_ref[k]
        high = own.astype(bf16)
        low = (own - high.astype(f32)).astype(bf16)
        around = jnp.dot(high, near, preferred_element_type=f32) + jnp.dot(low, near, preferred_element_type=f32)
        t_ref[k - 1] = t_ref[k - 1] - around

    def mix_slot(k):
        def block(ib, _):
            rows = pl.ds(pl.multiple_of(ib * IB, IB), IB)
            u = mixed(ib, r_ref[k])
            s_ref[k, rows] = weigh(b_ref[k], u)
            t_ref[k - 1, rows] = weigh(nb_ref[k - 1], u)
            return 0

        lax.fori_loop(0, NIB, block, 0)
        take_plane(k)

    def fill_differences(k):
        own = r_ref[k]
        behind = r_ref[k - 1].astype(f32)
        if k == 1:
            behind = behind * outer
            r_ref[0] = (own.astype(f32) - behind).astype(bf16)
        around = jnp.dot(own, near, preferred_element_type=f32)
        g_ref[...] = (6.0 * own.astype(f32) - around - behind - r_ref[k + 1].astype(f32)).astype(bf16)

    def finish_row(k):
        row = row_of(m, k)
        beside = 0 if k == 1 else k + 1
        other = 2 if k == 1 else k - 1

        def block(i, _):
            ib = lax.rem(m + 1 + i, GROUP)
            before = lax.rem(m + i, GROUP)

            @pl.when(i > 0)
            def _():
                modes = pl.ds(pl.multiple_of(before * IB, IB), IB)
                send(out_ref.at[k - 1, modes], img_ref.at[row], (d, before), back_sem.at[k - 1], home_sem.at[k - 1])

            rows = pl.ds(pl.multiple_of(ib * IB, IB), IB)
            u = mixed(ib, r_ref[beside])
            sums = weigh(b_ref[beside], u)
            if beside in (3, 4):
                s_ref[beside, rows] = sums
                t_ref[beside - 1, rows] = weigh(nb_ref[beside - 1], u)
            v = mixed(ib, g_ref[...])
            start = t_ref[k - 1, rows] - s_ref[other, rows]
            start = start + sums if k == 1 else start - sums
            total = weigh(b_ref[k], v, start).astype(bf16)
            out_ref[k - 1, rows] = total

            @pl.when(i == GROUP - 1)
            def _():
                img_ref[row] = total

            return 0

        lax.fori_loop(0, GROUP, block, 0)
        if beside in (3, 4):
            take_plane(beside)

    seven = pl.ds(0, GROUP - 1)
    drain(r_ref.at[1], recv_sem.at[1])
    mix_slot(1)

    @pl.when(odd)
    def _():
        pl.semaphore_wait(barrier, 2)
        for side in range(2):
            drain(pair_ref.at[side, pl.ds(0, 32)], pair_sem.at[2 + side])
        send(pair_ref.at[1], edge_ref.at[0], (up, m), edge_sem.at[0], edge_sem.at[2])
        send(pair_ref.at[0], edge_ref.at[1], (down, m), edge_sem.at[1], edge_sem.at[3])
        send(ce_ref.at[1], ch_ref.at[0], (up, m), coef_sem.at[0], coef_sem.at[2])
        send(ce_ref.at[0], ch_ref.at[1], (down, m), coef_sem.at[1], coef_sem.at[3])

    drain(r_ref.at[2], recv_sem.at[2])
    mix_slot(2)
    sent(3)
    issue(0)
    drain(r_ref.at[3], recv_sem.at[3])
    fill_differences(2)
    finish_row(2)

    both_modes = pl.ds(pl.multiple_of((m // 2) * 64, 64), 64)

    @pl.when(odd)
    def _():
        for side, holder in ((0, 0), (1, GROUP - 1)):
            drain(edge_ref.at[side], edge_sem.at[2 + side])

            @pl.when(m == holder)
            def _():
                pltpu.make_async_copy(edge_ref.at[side], r_ref.at[0, both_modes], recv_sem.at[0]).start()

            @pl.when(m != holder)
            def _():
                send(edge_ref.at[side], r_ref.at[0, both_modes], (d, holder), pair_sem.at[4 + side], recv_sem.at[0])

        for side in range(2):
            drain(ch_ref.at[side], coef_sem.at[2 + side])
        send(ch_ref, ch_ref, (d, sibling), coef_sem.at[4], coef_sem.at[5])

    drain(r_ref.at[4], recv_sem.at[4])
    forward = send(r_ref.at[4], r_ref.at[5], (d, sibling), send_sem.at[5], recv_sem.at[5])
    fill_differences(3)
    finish_row(3)

    @pl.when(even)
    def _():
        drain(ch_ref, coef_sem.at[5])

    row = row_of(m, 0)
    inside = coef_row(jnp.minimum(jnp.maximum(row, 0), 31))
    edge_coef = jnp.where(m == 0, ch_ref[0], jnp.where(m == GROUP - 1, ch_ref[1], inside))
    b_ref[0] = 0.5 * outer * edge_coef
    drain(r_ref.at[0], recv_sem.at[0])
    fill_differences(1)
    finish_row(1)

    row = iota((32, CELLS), 0)
    mean = mean_ref[...]
    c0_ref[0] = jnp.where(row == 0, ch_ref[0, 0:1] * first_edge, pltpu.roll(mean, 1, 0))
    c0_ref[1] = mean
    c0_ref[2] = jnp.where(row == 31, ch_ref[1, 0:1] * last_edge, pltpu.roll(mean, 31, 0))
    fill_faces(c0_ref, w_ref, inv_ref)
    forward.wait_recv()
    fill_differences(4)
    finish_row(4)

    loads[5].wait()
    drain(img_ref.at[seven], home_sem.at[0])
    first_inv = inv_ref[...] * (1.0 / cheb_center)
    for side, row in ((0, 0), (1, 31)):
        fe_ref[side] = (src_ref[:, row, :] - img_ref[row].astype(f32)) * first_inv[row : row + 1]
    swap = swap_matrix(16, 32)
    firsts = [
        send(fe_ref.at[1], fh_ref.at[0], (up, m), first_sem.at[0], first_sem.at[2]),
        send(fe_ref.at[0], fh_ref.at[1], (down, m), first_sem.at[1], first_sem.at[3]),
    ]
    for k in range(1, 4):
        drain(img_ref.at[seven], home_sem.at[k])
    for g in range(2):
        block = img_ref[:, 16 * g : 16 * (g + 1), :].reshape(512, CELLS)
        turned = jnp.dot(swap, block, preferred_element_type=f32).astype(bf16)
        nat_ref[16 * g : 16 * (g + 1)] = turned.reshape(16, 32, CELLS)

    @pl.when(odd)
    def _():
        for side, holder in ((0, 0), (1, GROUP - 1)):
            drain(edge_ref.at[side], edge_sem.at[side])
            drain(ce_ref.at[side], coef_sem.at[side])

            @pl.when(m != holder)
            def _():
                drain(edge_ref.at[side], pair_sem.at[4 + side])

        drain(ch_ref, coef_sem.at[4])

    @pl.when(even)
    def _():
        for side in range(2):
            drain(pair_ref.at[side, pl.ds(0, 32)], pair_sem.at[side])

    outermost = (m == 0) | (m == GROUP - 1)

    @pl.when(outermost)
    def _():
        drain(r_ref.at[1, pl.ds(0, 32 * (GROUP - 2))], send_sem.at[0])

    @pl.when(jnp.logical_not(outermost))
    def _():
        drain(r_ref.at[1, pl.ds(0, 32 * (GROUP - 3))], send_sem.at[0])

    sent(4)
    forward.wait_send()
    for k in range(4):
        drain(out_ref.at[k, pl.ds(0, 32 * (GROUP - 1))], back_sem.at[k])
    for copy in firsts:
        copy.wait_send()
        copy.wait_recv()
    halo_ref[0] = fh_ref[0] * first_edge
    halo_ref[1] = fh_ref[1] * last_edge


STEP = 8


def correct_kernel(it_ref, src_ref, nat_ref, halo_ref, w_ref, inv_ref, upd_ref, res_ref):
    row = iota((32, CELLS), 0)

    def update(mode, _):
        res = src_ref[mode] - nat_ref[mode].astype(f32)
        res_ref[mode] = res
        inv = inv_ref[...]
        first = res * inv * (1.0 / cheb_center)
        above = jnp.where(row == 31, halo_ref[1, pl.ds(mode, 1), :], pltpu.roll(first, 31, 0))
        below = jnp.where(row == 0, halo_ref[0, pl.ds(mode, 1), :], pltpu.roll(first, 1, 0))
        around = w_ref[0] * above + w_ref[1] * below
        for f, amount in enumerate((CELLS - NZ, NZ, CELLS - 1, 1)):
            around = around + w_ref[2 + f] * pltpu.roll(first, amount, 1)
        smoothed = res * (1.0 - 1.0 / cheb_center) + around
        second = rho_one * rho_zero * first + (2.0 * rho_one / cheb_radius) * smoothed * inv
        upd_ref[mode] = it_ref[mode] + first + second
        return 0

    lax.fori_loop(0, STEP, update, 0, unroll=2)


def body(iterate, source, mean_coef, kl_fields, tri_index, tri_value):
    sds = jax.ShapeDtypeStruct
    vm = pl.BlockSpec(memory_space=pltpu.VMEM)
    hbm = pl.BlockSpec(memory_space=pltpu.HBM)
    dma = pltpu.SemaphoreType.DMA
    natural, halo, w, inv = pl.pallas_call(
        exchange_kernel,
        out_shape=(
            sds((32, 32, CELLS), bf16),
            sds((2, 32, CELLS), f32),
            sds((6, 32, CELLS), f32),
            sds((32, CELLS), f32),
        ),
        in_specs=[hbm] * 6,
        out_specs=(vm, vm, vm, vm),
        scratch_shapes=[
            pltpu.VMEM((32, 32, CELLS), f32),
            pltpu.VMEM((32, 32, CELLS), f32),
            pltpu.VMEM((32, CELLS), f32),
            pltpu.VMEM((NF - 1, 32, CELLS), f32),
            pltpu.VMEM((3, ENTRIES), i32),
            pltpu.VMEM((42, 128), f32),
            pltpu.VMEM((32, 32, CELLS), bf16),
            pltpu.VMEM((2, 64, CELLS), bf16),
            pltpu.VMEM((2, 64, CELLS), bf16),
            pltpu.VMEM((6, P_SIZE, CELLS), bf16),
            pltpu.VMEM((NIB, NF * IB, P_SIZE), bf16),
            pltpu.VMEM((P_SIZE, 64), f32),
            pltpu.VMEM((P_SIZE, CELLS), bf16),
            pltpu.VMEM((6, 24, CELLS), f32),
            pltpu.VMEM((4, 24, CELLS), f32),
            pltpu.VMEM((6, P_SIZE, CELLS), f32),
            pltpu.VMEM((4, P_SIZE, CELLS), f32),
            pltpu.VMEM((2, 24, CELLS), f32),
            pltpu.VMEM((2, 24, CELLS), f32),
            pltpu.VMEM((4, P_SIZE, CELLS), bf16),
            pltpu.VMEM((32, 32, CELLS), bf16),
            pltpu.VMEM((2, 32, CELLS), f32),
            pltpu.VMEM((2, 32, CELLS), f32),
            pltpu.VMEM((3, 32, CELLS), f32),
            dma((6,)),
            dma((4,)),
            dma((6,)),
            dma((6,)),
            dma((6,)),
            dma((4,)),
            dma((4,)),
            dma((4,)),
            dma((6,)),
            pltpu.SemaphoreType.REGULAR,
        ],
        compiler_params=pltpu.CompilerParams(
            collective_id=0, has_side_effects=True, vmem_limit_bytes=50 * 2**20
        ),
    )(*[
        pltpu.with_memory_space_constraint(x, pltpu.HBM)
        for x in (iterate, source, mean_coef, kl_fields, tri_index.T, tri_value.reshape(42, 128))
    ])

    big = pl.BlockSpec((STEP, 32, CELLS), lambda g: (g, 0, 0))
    return pl.pallas_call(
        correct_kernel,
        out_shape=(sds((32, 32, CELLS), f32), sds((32, 32, CELLS), f32)),
        grid=(32 // STEP,),
        in_specs=[
            big,
            big,
            big,
            pl.BlockSpec((2, STEP, CELLS), lambda g: (0, g, 0)),
            pl.BlockSpec((6, 32, CELLS), lambda g: (0, 0, 0)),
            pl.BlockSpec((32, CELLS), lambda g: (0, 0)),
        ],
        out_specs=(big, big),
        compiler_params=pltpu.CompilerParams(vmem_limit_bytes=16 * 2**20),
    )(iterate, source, natural, halo, w, inv)


def solution(mesh):
    return jax.shard_map(
        body,
        mesh=mesh,
        in_specs=(
            P("mode", "dom", None),
            P("mode", "dom", None),
            P("dom", None),
            P(None, "dom", None),
            P(),
            P(),
        ),
        out_specs=(P("mode", "dom", None), P("mode", "dom", None)),
        check_vma=False,
    )
```

```python
import jax
import jax.numpy as jnp
from jax import lax
from jax.experimental import pallas as pl
from jax.experimental.pallas import tpu as pltpu
from jax.sharding import PartitionSpec as P

P_SIZE = 256
NF = 21
NZ = 16
CELLS = 256
IB = 64
NIB = P_SIZE // IB
SUB = 16
PER = IB // 32
ENTRIES = P_SIZE * NF

cheb_center = 1.125
cheb_radius = 0.875
sigma = cheb_center / cheb_radius
rho_zero = 1.0 / sigma
rho_one = 1.0 / (2.0 * sigma - rho_zero)

f32 = jnp.float32
bf16 = jnp.bfloat16
i32 = jnp.int32


def iota(shape, dim):
    return lax.broadcasted_iota(i32, shape, dim)


def plane_neighbours():
    q = iota((CELLS, CELLS), 0)
    p = iota((CELLS, CELLS), 1)
    far = jnp.abs(q - p)
    same = (q >> 4) == (p >> 4)
    return jnp.where((far == NZ) | ((far == 1) & same), 1.0, 0.0).astype(bf16)


def fill_table(tri_ref, val_ref, table_ref):
    mode = iota((P_SIZE, 256), 0)
    level = iota((32, 256), 0)

    def gather(step, total):
        here = pl.ds(pl.multiple_of(step * 256, 256), 256)
        worth = jnp.concatenate([val_ref[pl.ds(2 * step, 1)], val_ref[pl.ds(2 * step + 1, 1)]], 1)
        hot = jnp.where(mode == tri_ref[0:1, here], 1.0, 0.0).astype(bf16)
        mine = level == tri_ref[2:3, here]
        coef = jnp.where(mine, worth, 0.0).astype(bf16)
        trial = jnp.where(mine, tri_ref[1:2, here].astype(f32), 0.0).astype(bf16)
        both = jnp.concatenate([coef, trial], 0)
        return total + lax.dot_general(
            hot, both, (((1,), (1,)), ((), ())), preferred_element_type=f32
        )

    table_ref[...] = lax.fori_loop(0, ENTRIES // 256, gather, jnp.zeros((P_SIZE, 64), f32))


def fill_mixing(table_ref, mix_ref):
    column = iota((P_SIZE, P_SIZE), 1).astype(f32)
    for l in range(NF):
        coef = table_ref[:, l : l + 1]
        trial = table_ref[:, 32 + l : 33 + l]
        panel = jnp.where(column == trial, coef, 0.0).astype(bf16)
        mix_ref[:, l * IB : (l + 1) * IB, :] = panel.reshape(NIB, IB, P_SIZE)


def swap_matrix(major, minor):
    n = major * minor
    r = iota((n, n), 0)
    c = iota((n, n), 1)
    shift = minor.bit_length() - 1
    wanted = (r & (minor - 1)) * major + (r >> shift)
    return jnp.where(c == wanted, 1.0, 0.0).astype(bf16)


def lane_neighbours(x, z_place, place):
    up = jnp.where(z_place < NZ - 1, pltpu.roll(x, CELLS - 1, x.ndim - 1), 0.0)
    down = jnp.where(z_place > 0, pltpu.roll(x, 1, x.ndim - 1), 0.0)
    far = jnp.where(place < CELLS - NZ, pltpu.roll(x, CELLS - NZ, x.ndim - 1), 0.0)
    near = jnp.where(place >= NZ, pltpu.roll(x, NZ, x.ndim - 1), 0.0)
    return up + down + far + near


def fill_faces(c0_ref, w_ref, inv_ref):
    place = iota((32, CELLS), 1)
    z_place = place & (NZ - 1)
    c = c0_ref[1]
    w_ref[0] = 0.5 * (c + c0_ref[2])
    w_ref[1] = 0.5 * (c + c0_ref[0])
    diag = w_ref[0] + w_ref[1]
    tests = ((CELLS - NZ, place < CELLS - NZ), (NZ, place >= NZ), (CELLS - 1, z_place < NZ - 1), (1, z_place > 0))
    for f, (amount, inside) in enumerate(tests):
        w = 0.5 * (c + jnp.where(inside, pltpu.roll(c, amount, 1), 0.0))
        diag = diag + w
        w_ref[2 + f] = jnp.where(inside, w, 0.0)
    inv = 1.0 / diag
    weight = (2.0 * rho_one / cheb_radius) * inv
    for f in range(6):
        w_ref[f] = w_ref[f] * weight
    inv_ref[0] = inv * (1.0 / cheb_center)
    inv_ref[1] = inv * ((1.0 + rho_one * rho_zero) / cheb_center) + weight * (1.0 - 1.0 / cheb_center)


MESH = pl.DeviceIdType.MESH
GROUP = 8


def row_of(device, k):
    core = lax.rem(device, 2)
    return 8 * (device // 2) + core * (8 - k) + (1 - core) * (k - 1)


def exchange_kernel(
    it_hbm, src_hbm, mean_hbm, kl_hbm, tri_hbm, val_hbm, nat_ref, halo_ref, w_ref, inv_ref,
    it_ref, src_ref, mean_ref, kl_ref, tri_ref, val_ref, rows_ref, pair_ref, edge_ref, r_ref, mix_ref, table_ref, g_ref, b_ref, nb_ref, s_ref, t_ref, u_ref, v_ref,
    ce_ref, ch_ref, out_ref, img_ref, fe_ref, fh_ref, c0_ref,
    local_sem, edge_sem, send_sem, recv_sem, coef_sem, back_sem, home_sem, first_sem, pair_sem, go_sem,
):
    d = lax.axis_index("dom")
    m = lax.axis_index("mode")
    count = lax.axis_size("dom")
    up = lax.rem(d + 1, count)
    down = lax.rem(d + count - 1, count)
    sibling = m + 1 - 2 * lax.rem(m, 2)
    peers = [lax.rem(m + p, GROUP) for p in range(1, GROUP)]
    own_modes = pl.ds(pl.multiple_of(m * 32, 32), 32)

    def send(source, target, device, sent, got):
        copy = pltpu.make_async_remote_copy(
            src_ref=source, dst_ref=target, send_sem=sent, recv_sem=got, device_id=device, device_id_type=MESH
        )
        copy.start()
        return copy

    def drain(ref, sem):
        pltpu.make_async_copy(ref, ref, sem).wait()

    loads = [
        pltpu.make_async_copy(a, b, local_sem.at[i])
        for i, (a, b) in enumerate(
            (
                (it_hbm, it_ref),
                (kl_hbm, kl_ref),
                (mean_hbm, mean_ref),
                (tri_hbm, tri_ref),
                (val_hbm, val_ref),
                (src_hbm, src_ref),
            )
        )
    ]
    for load in loads:
        load.start()
    even = lax.rem(m, 2) == 0
    odd = lax.rem(m, 2) == 1
    barrier = pltpu.get_barrier_semaphore()
    for peer in peers:

        @pl.when(lax.rem(peer, 2) == 0)
        def _():
            pl.semaphore_signal(barrier, inc=1, device_id=(d, peer), device_id_type=MESH)

    @pl.when(odd)
    def _():
        for other in (up, down):
            pl.semaphore_signal(barrier, inc=1, device_id=(other, m), device_id_type=MESH)

    loads[0].wait()
    swap = swap_matrix(32, 16)
    for g in range(2):
        block = it_ref[16 * g : 16 * (g + 1)].astype(bf16).reshape(512, CELLS)
        turned = jnp.dot(swap, block, preferred_element_type=f32).astype(bf16)
        rows_ref[:, 16 * g : 16 * (g + 1), :] = turned.reshape(32, 16, CELLS)
    pair_ref[0, 32:64] = rows_ref[0]
    pair_ref[1, 32:64] = rows_ref[31]
    loads[1].wait()
    loads[2].wait()
    blank = jnp.zeros((3, CELLS), f32)
    for side, row in ((0, 0), (1, 31)):
        ce_ref[side] = jnp.concatenate([mean_ref[row : row + 1], kl_ref[:, row, :], blank], 0)

    @pl.when(even)
    def _():
        pl.semaphore_wait(barrier, GROUP - 1)
        pl.semaphore_signal(go_sem, inc=1, device_id=(d, sibling), device_id_type=MESH)

    @pl.when(odd)
    def _():
        pl.semaphore_wait(go_sem, 1)

    def issue(k):
        for peer in peers:
            row = row_of(peer, k)

            def pass_row():
                send(rows_ref.at[row], r_ref.at[k, own_modes], (d, peer), send_sem.at[k], recv_sem.at[k])

            if k > 0:
                pass_row()
            else:
                pl.when((row >= 0) & (row < 32))(pass_row)
        row = row_of(m, k)

        def keep_row():
            pltpu.make_async_copy(rows_ref.at[row], r_ref.at[k, own_modes], recv_sem.at[k]).start()

        if k > 0:
            keep_row()
        else:
            pl.when((row >= 0) & (row < 32))(keep_row)

    def sent(k):
        drain(r_ref.at[k, pl.ds(0, 32 * (GROUP - 1))], send_sem.at[k])

    @pl.when(even)
    def _():
        for side, row in ((0, 0), (1, 31)):
            send(rows_ref.at[row], pair_ref.at[side, pl.ds(0, 32)], (d, sibling), pair_sem.at[side], pair_sem.at[2 + side])

    issue(1)
    issue(2)
    loads[3].wait()
    loads[4].wait()
    fill_table(tri_ref, val_ref, table_ref)
    sent(1)
    issue(3)
    fill_mixing(table_ref, mix_ref)

    first_edge = jnp.where(d == 0, 0.0, 1.0)
    last_edge = jnp.where(d == count - 1, 0.0, 1.0)
    outer = jnp.where(m == 0, first_edge, jnp.where(m == GROUP - 1, last_edge, 1.0))

    def coef_row(row):
        kl_row = kl_ref[:, pl.ds(row, 1), :].reshape(NF - 1, CELLS)
        return jnp.concatenate([mean_ref[pl.ds(row, 1), :], kl_row, blank], 0)

    for k in range(1, 6):
        b_ref[k] = 0.5 * coef_row(row_of(m, k))
    place = iota((24, CELLS), 1)
    for k in range(1, 5):
        beside = b_ref[k + 1] if k == 1 else b_ref[k - 1] + b_ref[k + 1]
        nb_ref[k - 1] = beside + lane_neighbours(b_ref[k], place & (NZ - 1), place)
    near = plane_neighbours()
    sent(2)
    issue(4)

    def mixed(ib, panel, into):
        into[...] = jnp.dot(mix_ref[ib], panel, preferred_element_type=f32)

    def weigh(pairs, source, q, totals):
        totals = list(totals)
        for l in range(NF):
            piece = source[l * IB + q : l * IB + q + SUB]
            for n, coef in enumerate(pairs):
                term = coef[l : l + 1] * piece
                totals[n] = term if totals[n] is None else totals[n] + term
        return totals

    def take_plane(k):
        own = s_ref[k]
        high = own.astype(bf16)
        low = (own - high.astype(f32)).astype(bf16)
        around = jnp.dot(high, near, preferred_element_type=f32) + jnp.dot(low, near, preferred_element_type=f32)
        t_ref[k - 1] = t_ref[k - 1] - around

    def mix_slot(k):
        def block(ib, _):
            mixed(ib, r_ref[k], u_ref)
            for q in range(0, IB, SUB):
                here = pl.ds(pl.multiple_of(ib * IB + q, SUB), SUB)
                s_ref[k, here], t_ref[k - 1, here] = weigh((b_ref.at[k], nb_ref.at[k - 1]), u_ref, q, (None, None))
            return 0

        lax.fori_loop(0, NIB, block, 0)
        take_plane(k)

    def fill_differences(k):
        own = r_ref[k]
        behind = r_ref[k - 1].astype(f32)
        if k == 1:
            behind = behind * outer
            r_ref[0] = (own.astype(f32) - behind).astype(bf16)
        around = jnp.dot(own, near, preferred_element_type=f32)
        g_ref[...] = (6.0 * own.astype(f32) - around - behind - r_ref[k + 1].astype(f32)).astype(bf16)

    def finish_row(k):
        row = row_of(m, k)
        beside = 0 if k == 1 else k + 1
        other = 2 if k == 1 else k - 1

        def pass_on(device):
            modes = pl.ds(pl.multiple_of(device * 32, 32), 32)
            send(out_ref.at[k - 1, modes], img_ref.at[row], (d, device), back_sem.at[k - 1], home_sem.at[k - 1])

        def block(i, _):
            ib = lax.rem(m // PER + 1 + i, NIB)
            before = lax.rem(m // PER + i, NIB)

            @pl.when(i > 0)
            def _():
                for q in range(PER):
                    pass_on(PER * before + q)

            mixed(ib, r_ref[beside], u_ref)
            mixed(ib, g_ref[...], v_ref)
            for q in range(0, IB, SUB):
                here = pl.ds(pl.multiple_of(ib * IB + q, SUB), SUB)
                start = t_ref[k - 1, here] - s_ref[other, here]
                if beside in (3, 4):
                    sums, extra = weigh((b_ref.at[beside], nb_ref.at[beside - 1]), u_ref, q, (None, None))
                    s_ref[beside, here] = sums
                    t_ref[beside - 1, here] = extra
                else:
                    (sums,) = weigh((b_ref.at[beside],), u_ref, q, (None,))
                start = start + sums if k == 1 else start - sums
                (total,) = weigh((b_ref.at[k],), v_ref, q, (start,))
                out_ref[k - 1, here] = total.astype(bf16)
            return 0

        lax.fori_loop(0, NIB, block, 0)
        if beside in (3, 4):
            take_plane(beside)
        img_ref[row] = out_ref[k - 1, own_modes]

        def rest():
            for q in range(1, PER):
                pass_on(PER * (m // PER) + lax.rem(m + q, PER))

        return rest

    seven = pl.ds(0, GROUP - 1)
    drain(r_ref.at[1], recv_sem.at[1])
    mix_slot(1)

    @pl.when(odd)
    def _():
        pl.semaphore_wait(barrier, 2)
        for side in range(2):
            drain(pair_ref.at[side, pl.ds(0, 32)], pair_sem.at[2 + side])
        send(pair_ref.at[1], edge_ref.at[0], (up, m), edge_sem.at[0], edge_sem.at[2])
        send(pair_ref.at[0], edge_ref.at[1], (down, m), edge_sem.at[1], edge_sem.at[3])
        send(ce_ref.at[1], ch_ref.at[0], (up, m), coef_sem.at[0], coef_sem.at[2])
        send(ce_ref.at[0], ch_ref.at[1], (down, m), coef_sem.at[1], coef_sem.at[3])

    drain(r_ref.at[2], recv_sem.at[2])
    mix_slot(2)
    sent(3)
    issue(0)
    drain(r_ref.at[3], recv_sem.at[3])
    fill_differences(2)
    finish_row(2)()

    both_modes = pl.ds(pl.multiple_of((m // 2) * 64, 64), 64)

    @pl.when(odd)
    def _():
        for side, holder in ((0, 0), (1, GROUP - 1)):
            drain(edge_ref.at[side], edge_sem.at[2 + side])

            @pl.when(m == holder)
            def _():
                pltpu.make_async_copy(edge_ref.at[side], r_ref.at[0, both_modes], recv_sem.at[0]).start()

            @pl.when(m != holder)
            def _():
                send(edge_ref.at[side], r_ref.at[0, both_modes], (d, holder), pair_sem.at[4 + side], recv_sem.at[0])

        for side in range(2):
            drain(ch_ref.at[side], coef_sem.at[2 + side])
        send(ch_ref, ch_ref, (d, sibling), coef_sem.at[4], coef_sem.at[5])

    drain(r_ref.at[4], recv_sem.at[4])
    forward = send(r_ref.at[4], r_ref.at[5], (d, sibling), send_sem.at[5], recv_sem.at[5])
    fill_differences(3)
    finish_row(3)()

    @pl.when(even)
    def _():
        drain(ch_ref, coef_sem.at[5])

    row = row_of(m, 0)
    inside = coef_row(jnp.minimum(jnp.maximum(row, 0), 31))
    edge_coef = jnp.where(m == 0, ch_ref[0], jnp.where(m == GROUP - 1, ch_ref[1], inside))
    b_ref[0] = 0.5 * outer * edge_coef
    drain(r_ref.at[0], recv_sem.at[0])
    fill_differences(1)
    last = finish_row(1)

    row = iota((32, CELLS), 0)
    mean = mean_ref[...]
    c0_ref[0] = jnp.where(row == 0, ch_ref[0, 0:1] * first_edge, pltpu.roll(mean, 1, 0))
    c0_ref[1] = mean
    c0_ref[2] = jnp.where(row == 31, ch_ref[1, 0:1] * last_edge, pltpu.roll(mean, 31, 0))
    fill_faces(c0_ref, w_ref, inv_ref)
    last()
    forward.wait_recv()
    fill_differences(4)
    last = finish_row(4)
    loads[5].wait()
    last()
    drain(img_ref.at[seven], home_sem.at[0])
    first_inv = inv_ref[0]
    for side, row in ((0, 0), (1, 31)):
        fe_ref[side] = (src_ref[:, row, :] - img_ref[row].astype(f32)) * first_inv[row : row + 1]
    swap = swap_matrix(16, 32)
    firsts = [
        send(fe_ref.at[1], fh_ref.at[0], (up, m), first_sem.at[0], first_sem.at[2]),
        send(fe_ref.at[0], fh_ref.at[1], (down, m), first_sem.at[1], first_sem.at[3]),
    ]
    for k in range(1, 4):
        drain(img_ref.at[seven], home_sem.at[k])
    for g in range(2):
        block = img_ref[:, 16 * g : 16 * (g + 1), :].reshape(512, CELLS)
        turned = jnp.dot(swap, block, preferred_element_type=f32).astype(bf16)
        nat_ref[16 * g : 16 * (g + 1)] = turned.reshape(16, 32, CELLS)

    @pl.when(odd)
    def _():
        for side, holder in ((0, 0), (1, GROUP - 1)):
            drain(edge_ref.at[side], edge_sem.at[side])
            drain(ce_ref.at[side], coef_sem.at[side])

            @pl.when(m != holder)
            def _():
                drain(edge_ref.at[side], pair_sem.at[4 + side])

        drain(ch_ref, coef_sem.at[4])

    @pl.when(even)
    def _():
        for side in range(2):
            drain(pair_ref.at[side, pl.ds(0, 32)], pair_sem.at[side])

    outermost = (m == 0) | (m == GROUP - 1)

    @pl.when(outermost)
    def _():
        drain(r_ref.at[1, pl.ds(0, 32 * (GROUP - 2))], send_sem.at[0])

    @pl.when(jnp.logical_not(outermost))
    def _():
        drain(r_ref.at[1, pl.ds(0, 32 * (GROUP - 3))], send_sem.at[0])

    sent(4)
    forward.wait_send()
    for k in range(4):
        drain(out_ref.at[k, pl.ds(0, 32 * (GROUP - 1))], back_sem.at[k])
    for copy in firsts:
        copy.wait_send()
        copy.wait_recv()
    halo_ref[0] = fh_ref[0] * first_edge
    halo_ref[1] = fh_ref[1] * last_edge


STEP = 8


def correct_kernel(it_ref, src_ref, nat_ref, halo_ref, w_ref, inv_ref, upd_ref, res_ref):
    row = iota((32, CELLS), 0)

    def update(mode, _):
        res = src_ref[mode] - nat_ref[mode].astype(f32)
        res_ref[mode] = res
        first = res * inv_ref[0]
        total = it_ref[mode] + res * inv_ref[1]
        for f, amount in enumerate((CELLS - NZ, NZ, CELLS - 1, 1)):
            total = total + w_ref[2 + f] * pltpu.roll(first, amount, 1)
        above = jnp.where(row == 31, halo_ref[1, pl.ds(mode, 1), :], pltpu.roll(first, 31, 0))
        below = jnp.where(row == 0, halo_ref[0, pl.ds(mode, 1), :], pltpu.roll(first, 1, 0))
        upd_ref[mode] = total + w_ref[0] * above + w_ref[1] * below
        return 0

    lax.fori_loop(0, STEP, update, 0, unroll=4)


def body(iterate, source, mean_coef, kl_fields, tri_index, tri_value):
    sds = jax.ShapeDtypeStruct
    vm = pl.BlockSpec(memory_space=pltpu.VMEM)
    hbm = pl.BlockSpec(memory_space=pltpu.HBM)
    dma = pltpu.SemaphoreType.DMA
    natural, halo, w, inv = pl.pallas_call(
        exchange_kernel,
        out_shape=(
            sds((32, 32, CELLS), bf16),
            sds((2, 32, CELLS), f32),
            sds((6, 32, CELLS), f32),
            sds((2, 32, CELLS), f32),
        ),
        in_specs=[hbm] * 6,
        out_specs=(vm, vm, vm, vm),
        scratch_shapes=[
            pltpu.VMEM((32, 32, CELLS), f32),
            pltpu.VMEM((32, 32, CELLS), f32),
            pltpu.VMEM((32, CELLS), f32),
            pltpu.VMEM((NF - 1, 32, CELLS), f32),
            pltpu.VMEM((3, ENTRIES), i32),
            pltpu.VMEM((42, 128), f32),
            pltpu.VMEM((32, 32, CELLS), bf16),
            pltpu.VMEM((2, 64, CELLS), bf16),
            pltpu.VMEM((2, 64, CELLS), bf16),
            pltpu.VMEM((6, P_SIZE, CELLS), bf16),
            pltpu.VMEM((NIB, NF * IB, P_SIZE), bf16),
            pltpu.VMEM((P_SIZE, 64), f32),
            pltpu.VMEM((P_SIZE, CELLS), bf16),
            pltpu.VMEM((6, 24, CELLS), f32),
            pltpu.VMEM((4, 24, CELLS), f32),
            pltpu.VMEM((6, P_SIZE, CELLS), f32),
            pltpu.VMEM((4, P_SIZE, CELLS), f32),
            pltpu.VMEM((NF * IB, CELLS), f32),
            pltpu.VMEM((NF * IB, CELLS), f32),
            pltpu.VMEM((2, 24, CELLS), f32),
            pltpu.VMEM((2, 24, CELLS), f32),
            pltpu.VMEM((4, P_SIZE, CELLS), bf16),
            pltpu.VMEM((32, 32, CELLS), bf16),
            pltpu.VMEM((2, 32, CELLS), f32),
            pltpu.VMEM((2, 32, CELLS), f32),
            pltpu.VMEM((3, 32, CELLS), f32),
            dma((6,)),
            dma((4,)),
            dma((6,)),
            dma((6,)),
            dma((6,)),
            dma((4,)),
            dma((4,)),
            dma((4,)),
            dma((6,)),
            pltpu.SemaphoreType.REGULAR,
        ],
        compiler_params=pltpu.CompilerParams(
            collective_id=0, has_side_effects=True, vmem_limit_bytes=50 * 2**20
        ),
    )(*[
        pltpu.with_memory_space_constraint(x, pltpu.HBM)
        for x in (iterate, source, mean_coef, kl_fields, tri_index.T, tri_value.reshape(42, 128))
    ])

    big = pl.BlockSpec((STEP, 32, CELLS), lambda g: (g, 0, 0))
    return pl.pallas_call(
        correct_kernel,
        out_shape=(sds((32, 32, CELLS), f32), sds((32, 32, CELLS), f32)),
        grid=(32 // STEP,),
        in_specs=[
            big,
            big,
            big,
            pl.BlockSpec((2, STEP, CELLS), lambda g: (0, g, 0)),
            pl.BlockSpec((6, 32, CELLS), lambda g: (0, 0, 0)),
            pl.BlockSpec((2, 32, CELLS), lambda g: (0, 0, 0)),
        ],
        out_specs=(big, big),
        compiler_params=pltpu.CompilerParams(vmem_limit_bytes=16 * 2**20),
    )(iterate, source, natural, halo, w, inv)


def solution(mesh):
    return jax.shard_map(
        body,
        mesh=mesh,
        in_specs=(
            P("mode", "dom", None),
            P("mode", "dom", None),
            P("dom", None),
            P(None, "dom", None),
            P(),
            P(),
        ),
        out_specs=(P("mode", "dom", None), P("mode", "dom", None)),
        check_vma=False,
    )
```

```python
import jax
import jax.numpy as jnp
from jax import lax
from jax.experimental import pallas as pl
from jax.experimental.pallas import tpu as pltpu
from jax.sharding import PartitionSpec as P

P_SIZE = 256
NF = 21
NZ = 16
CELLS = 256
IB = 64
NIB = P_SIZE // IB
SUB = 16
PER = IB // 32
ENTRIES = P_SIZE * NF

cheb_center = 1.125
cheb_radius = 0.875
sigma = cheb_center / cheb_radius
rho_zero = 1.0 / sigma
rho_one = 1.0 / (2.0 * sigma - rho_zero)

f32 = jnp.float32
bf16 = jnp.bfloat16
i32 = jnp.int32


def iota(shape, dim):
    return lax.broadcasted_iota(i32, shape, dim)


def plane_neighbours():
    q = iota((CELLS, CELLS), 0)
    p = iota((CELLS, CELLS), 1)
    far = jnp.abs(q - p)
    same = (q >> 4) == (p >> 4)
    return jnp.where((far == NZ) | ((far == 1) & same), 1.0, 0.0).astype(bf16)


def fill_table(tri_ref, val_ref, table_ref):
    mode = iota((P_SIZE, 256), 0)
    level = iota((32, 256), 0)

    def gather(step, total):
        here = pl.ds(pl.multiple_of(step * 256, 256), 256)
        worth = jnp.concatenate([val_ref[pl.ds(2 * step, 1)], val_ref[pl.ds(2 * step + 1, 1)]], 1)
        hot = jnp.where(mode == tri_ref[0:1, here], 1.0, 0.0).astype(bf16)
        mine = level == tri_ref[2:3, here]
        coef = jnp.where(mine, worth, 0.0).astype(bf16)
        trial = jnp.where(mine, tri_ref[1:2, here].astype(f32), 0.0).astype(bf16)
        both = jnp.concatenate([coef, trial], 0)
        return total + lax.dot_general(
            hot, both, (((1,), (1,)), ((), ())), preferred_element_type=f32
        )

    table_ref[...] = lax.fori_loop(0, ENTRIES // 256, gather, jnp.zeros((P_SIZE, 64), f32))


def fill_mixing(table_ref, mix_ref):
    column = iota((P_SIZE, P_SIZE), 1).astype(f32)
    for l in range(NF):
        coef = table_ref[:, l : l + 1]
        trial = table_ref[:, 32 + l : 33 + l]
        panel = jnp.where(column == trial, coef, 0.0).astype(bf16)
        mix_ref[:, l * IB : (l + 1) * IB, :] = panel.reshape(NIB, IB, P_SIZE)


def swap_matrix(major, minor):
    n = major * minor
    r = iota((n, n), 0)
    c = iota((n, n), 1)
    shift = minor.bit_length() - 1
    wanted = (r & (minor - 1)) * major + (r >> shift)
    return jnp.where(c == wanted, 1.0, 0.0).astype(bf16)


def lane_neighbours(x, z_place, place):
    up = jnp.where(z_place < NZ - 1, pltpu.roll(x, CELLS - 1, x.ndim - 1), 0.0)
    down = jnp.where(z_place > 0, pltpu.roll(x, 1, x.ndim - 1), 0.0)
    far = jnp.where(place < CELLS - NZ, pltpu.roll(x, CELLS - NZ, x.ndim - 1), 0.0)
    near = jnp.where(place >= NZ, pltpu.roll(x, NZ, x.ndim - 1), 0.0)
    return up + down + far + near


def fill_faces(c0_ref, w_ref, inv_ref):
    place = iota((32, CELLS), 1)
    z_place = place & (NZ - 1)
    c = c0_ref[1]
    w_ref[0] = 0.5 * (c + c0_ref[2])
    w_ref[1] = 0.5 * (c + c0_ref[0])
    diag = w_ref[0] + w_ref[1]
    tests = ((CELLS - NZ, place < CELLS - NZ), (NZ, place >= NZ), (CELLS - 1, z_place < NZ - 1), (1, z_place > 0))
    for f, (amount, inside) in enumerate(tests):
        w = 0.5 * (c + jnp.where(inside, pltpu.roll(c, amount, 1), 0.0))
        diag = diag + w
        w_ref[2 + f] = jnp.where(inside, w, 0.0)
    inv = 1.0 / diag
    weight = (2.0 * rho_one / cheb_radius) * inv
    for f in range(6):
        w_ref[f] = w_ref[f] * weight
    inv_ref[0] = inv * (1.0 / cheb_center)
    inv_ref[1] = inv * ((1.0 + rho_one * rho_zero) / cheb_center) + weight * (1.0 - 1.0 / cheb_center)


MESH = pl.DeviceIdType.MESH
GROUP = 8


def row_of(device, k):
    core = lax.rem(device, 2)
    return 8 * (device // 2) + core * (8 - k) + (1 - core) * (k - 1)


def exchange_kernel(
    it_hbm, src_hbm, mean_hbm, kl_hbm, tri_hbm, val_hbm, nat_ref, halo_ref, w_ref, inv_ref,
    it_ref, src_ref, mean_ref, kl_ref, tri_ref, val_ref, rows_ref, pair_ref, r_ref, mix_ref, table_ref, g_ref, b_ref, nb_ref, s_ref, t_ref, u_ref, v_ref,
    ce_ref, ch_ref, out_ref, img_ref, fe_ref, fh_ref, c0_ref,
    local_sem, edge_sem, send_sem, recv_sem, coef_sem, back_sem, home_sem, first_sem, pair_sem, go_sem,
):
    d = lax.axis_index("dom")
    m = lax.axis_index("mode")
    count = lax.axis_size("dom")
    up = lax.rem(d + 1, count)
    down = lax.rem(d + count - 1, count)
    sibling = m + 1 - 2 * lax.rem(m, 2)
    peers = [lax.rem(m + p, GROUP) for p in range(1, GROUP)]
    own_modes = pl.ds(pl.multiple_of(m * 32, 32), 32)

    def send(source, target, device, sent, got):
        copy = pltpu.make_async_remote_copy(
            src_ref=source, dst_ref=target, send_sem=sent, recv_sem=got, device_id=device, device_id_type=MESH
        )
        copy.start()
        return copy

    def drain(ref, sem):
        pltpu.make_async_copy(ref, ref, sem).wait()

    loads = [
        pltpu.make_async_copy(a, b, local_sem.at[i])
        for i, (a, b) in enumerate(
            (
                (it_hbm, it_ref),
                (kl_hbm, kl_ref),
                (mean_hbm, mean_ref),
                (tri_hbm, tri_ref),
                (val_hbm, val_ref),
                (src_hbm, src_ref),
            )
        )
    ]
    for load in loads:
        load.start()
    even = lax.rem(m, 2) == 0
    odd = lax.rem(m, 2) == 1
    barrier = pltpu.get_barrier_semaphore()
    for peer in peers:

        @pl.when(lax.rem(peer, 2) == 0)
        def _():
            pl.semaphore_signal(barrier, inc=1, device_id=(d, peer), device_id_type=MESH)

    @pl.when(odd)
    def _():
        for other in (up, down):
            pl.semaphore_signal(barrier, inc=1, device_id=(other, m), device_id_type=MESH)

    for holder, other in ((0, down), (GROUP - 1, up)):

        @pl.when(m == holder)
        def _():
            for q in range(1, GROUP, 2):
                pl.semaphore_signal(barrier, inc=1, device_id=(other, q), device_id_type=MESH)

    loads[0].wait()
    swap = swap_matrix(32, 16)
    for g in range(2):
        block = it_ref[16 * g : 16 * (g + 1)].astype(bf16).reshape(512, CELLS)
        turned = jnp.dot(swap, block, preferred_element_type=f32).astype(bf16)
        rows_ref[:, 16 * g : 16 * (g + 1), :] = turned.reshape(32, 16, CELLS)
    pair_ref[0, 32:64] = rows_ref[0]
    pair_ref[1, 32:64] = rows_ref[31]
    loads[1].wait()
    loads[2].wait()
    blank = jnp.zeros((3, CELLS), f32)
    for side, row in ((0, 0), (1, 31)):
        ce_ref[side] = jnp.concatenate([mean_ref[row : row + 1], kl_ref[:, row, :], blank], 0)

    @pl.when(even)
    def _():
        pl.semaphore_wait(barrier, GROUP - 1)
        pl.semaphore_signal(go_sem, inc=1, device_id=(d, sibling), device_id_type=MESH)

    @pl.when(odd)
    def _():
        pl.semaphore_wait(go_sem, 1)

    def issue(k):
        for peer in peers:
            row = row_of(peer, k)

            def pass_row():
                send(rows_ref.at[row], r_ref.at[k, own_modes], (d, peer), send_sem.at[k], recv_sem.at[k])

            if k > 0:
                pass_row()
            else:
                pl.when((row >= 0) & (row < 32))(pass_row)
        row = row_of(m, k)

        def keep_row():
            pltpu.make_async_copy(rows_ref.at[row], r_ref.at[k, own_modes], recv_sem.at[k]).start()

        if k > 0:
            keep_row()
        else:
            pl.when((row >= 0) & (row < 32))(keep_row)

    def sent(k):
        drain(r_ref.at[k, pl.ds(0, 32 * (GROUP - 1))], send_sem.at[k])

    @pl.when(even)
    def _():
        for side, row in ((0, 0), (1, 31)):
            send(rows_ref.at[row], pair_ref.at[side, pl.ds(0, 32)], (d, sibling), pair_sem.at[side], pair_sem.at[2 + side])

    issue(1)
    issue(2)
    loads[3].wait()
    loads[4].wait()
    fill_table(tri_ref, val_ref, table_ref)
    sent(1)
    issue(3)
    fill_mixing(table_ref, mix_ref)

    first_edge = jnp.where(d == 0, 0.0, 1.0)
    last_edge = jnp.where(d == count - 1, 0.0, 1.0)
    outer = jnp.where(m == 0, first_edge, jnp.where(m == GROUP - 1, last_edge, 1.0))

    def coef_row(row):
        kl_row = kl_ref[:, pl.ds(row, 1), :].reshape(NF - 1, CELLS)
        return jnp.concatenate([mean_ref[pl.ds(row, 1), :], kl_row, blank], 0)

    for k in range(1, 6):
        b_ref[k] = 0.5 * coef_row(row_of(m, k))
    place = iota((24, CELLS), 1)
    for k in range(1, 5):
        beside = b_ref[k + 1] if k == 1 else b_ref[k - 1] + b_ref[k + 1]
        nb_ref[k - 1] = beside + lane_neighbours(b_ref[k], place & (NZ - 1), place)
    near = plane_neighbours()
    sent(2)
    issue(4)

    def mixed(ib, panel, into):
        into[...] = jnp.dot(mix_ref[ib], panel, preferred_element_type=f32)

    def weigh(pairs, source, q, totals):
        totals = list(totals)
        for l in range(NF):
            piece = source[l * IB + q : l * IB + q + SUB]
            for n, coef in enumerate(pairs):
                term = coef[l : l + 1] * piece
                totals[n] = term if totals[n] is None else totals[n] + term
        return totals

    def take_plane(k):
        own = s_ref[k]
        high = own.astype(bf16)
        low = (own - high.astype(f32)).astype(bf16)
        around = jnp.dot(high, near, preferred_element_type=f32) + jnp.dot(low, near, preferred_element_type=f32)
        t_ref[k - 1] = t_ref[k - 1] - around

    def mix_slot(k):
        def block(ib, _):
            mixed(ib, r_ref[k], u_ref)
            for q in range(0, IB, SUB):
                here = pl.ds(pl.multiple_of(ib * IB + q, SUB), SUB)
                s_ref[k, here], t_ref[k - 1, here] = weigh((b_ref.at[k], nb_ref.at[k - 1]), u_ref, q, (None, None))
            return 0

        lax.fori_loop(0, NIB, block, 0)
        take_plane(k)

    def fill_differences(k):
        own = r_ref[k]
        behind = r_ref[k - 1].astype(f32)
        if k == 1:
            behind = behind * outer
            r_ref[0] = (own.astype(f32) - behind).astype(bf16)
        around = jnp.dot(own, near, preferred_element_type=f32)
        g_ref[...] = (6.0 * own.astype(f32) - around - behind - r_ref[k + 1].astype(f32)).astype(bf16)

    def finish_row(k):
        row = row_of(m, k)
        beside = 0 if k == 1 else k + 1
        other = 2 if k == 1 else k - 1

        def pass_on(device):
            modes = pl.ds(pl.multiple_of(device * 32, 32), 32)
            send(out_ref.at[k - 1, modes], img_ref.at[row], (d, device), back_sem.at[k - 1], home_sem.at[k - 1])

        def block(i, _):
            ib = lax.rem(m // PER + 1 + i, NIB)
            before = lax.rem(m // PER + i, NIB)

            @pl.when(i > 0)
            def _():
                for q in range(PER):
                    pass_on(PER * before + q)

            mixed(ib, r_ref[beside], u_ref)
            mixed(ib, g_ref[...], v_ref)
            for q in range(0, IB, SUB):
                here = pl.ds(pl.multiple_of(ib * IB + q, SUB), SUB)
                start = t_ref[k - 1, here] - s_ref[other, here]
                if beside in (3, 4):
                    sums, extra = weigh((b_ref.at[beside], nb_ref.at[beside - 1]), u_ref, q, (None, None))
                    s_ref[beside, here] = sums
                    t_ref[beside - 1, here] = extra
                else:
                    (sums,) = weigh((b_ref.at[beside],), u_ref, q, (None,))
                start = start + sums if k == 1 else start - sums
                (total,) = weigh((b_ref.at[k],), v_ref, q, (start,))
                out_ref[k - 1, here] = total.astype(bf16)
            return 0

        lax.fori_loop(0, NIB, block, 0)
        if beside in (3, 4):
            take_plane(beside)
        img_ref[row] = out_ref[k - 1, own_modes]

        def rest():
            for q in range(1, PER):
                pass_on(PER * (m // PER) + lax.rem(m + q, PER))

        return rest

    both_modes = pl.ds(pl.multiple_of((m // 2) * 64, 64), 64)
    seven = pl.ds(0, GROUP - 1)
    drain(r_ref.at[1], recv_sem.at[1])
    mix_slot(1)

    @pl.when(odd)
    def _():
        pl.semaphore_wait(barrier, 4)
        for side in range(2):
            drain(pair_ref.at[side, pl.ds(0, 32)], pair_sem.at[2 + side])
        send(pair_ref.at[1], r_ref.at[0, both_modes], (up, 0), edge_sem.at[0], recv_sem.at[0])
        send(pair_ref.at[0], r_ref.at[0, both_modes], (down, GROUP - 1), edge_sem.at[1], recv_sem.at[0])
        send(ce_ref.at[1], ch_ref.at[0], (up, m), coef_sem.at[0], coef_sem.at[2])
        send(ce_ref.at[0], ch_ref.at[1], (down, m), coef_sem.at[1], coef_sem.at[3])

    drain(r_ref.at[2], recv_sem.at[2])
    mix_slot(2)
    sent(3)
    issue(0)
    drain(r_ref.at[3], recv_sem.at[3])
    fill_differences(2)
    finish_row(2)()

    @pl.when(odd)
    def _():
        for side in range(2):
            drain(ch_ref.at[side], coef_sem.at[2 + side])
        send(ch_ref, ch_ref, (d, sibling), coef_sem.at[4], coef_sem.at[5])

    drain(r_ref.at[4], recv_sem.at[4])
    forward = send(r_ref.at[4], r_ref.at[5], (d, sibling), send_sem.at[5], recv_sem.at[5])
    fill_differences(3)
    finish_row(3)()

    @pl.when(even)
    def _():
        drain(ch_ref, coef_sem.at[5])

    row = row_of(m, 0)
    inside = coef_row(jnp.minimum(jnp.maximum(row, 0), 31))
    edge_coef = jnp.where(m == 0, ch_ref[0], jnp.where(m == GROUP - 1, ch_ref[1], inside))
    b_ref[0] = 0.5 * outer * edge_coef
    drain(r_ref.at[0], recv_sem.at[0])
    fill_differences(1)
    last = finish_row(1)

    row = iota((32, CELLS), 0)
    mean = mean_ref[...]
    c0_ref[0] = jnp.where(row == 0, ch_ref[0, 0:1] * first_edge, pltpu.roll(mean, 1, 0))
    c0_ref[1] = mean
    c0_ref[2] = jnp.where(row == 31, ch_ref[1, 0:1] * last_edge, pltpu.roll(mean, 31, 0))
    fill_faces(c0_ref, w_ref, inv_ref)
    last()
    forward.wait_recv()
    fill_differences(4)
    last = finish_row(4)
    loads[5].wait()
    last()
    drain(img_ref.at[seven], home_sem.at[0])
    first_inv = inv_ref[0]
    for side, row in ((0, 0), (1, 31)):
        fe_ref[side] = (src_ref[:, row, :] - img_ref[row].astype(f32)) * first_inv[row : row + 1]
    swap = swap_matrix(16, 32)
    @pl.when(d < count - 1)
    def _():
        send(fe_ref.at[1], fh_ref.at[0], (up, m), first_sem.at[0], first_sem.at[2])

    @pl.when(d > 0)
    def _():
        send(fe_ref.at[0], fh_ref.at[1], (down, m), first_sem.at[1], first_sem.at[3])

    for k in range(1, 4):
        drain(img_ref.at[seven], home_sem.at[k])
    for g in range(2):
        block = img_ref[:, 16 * g : 16 * (g + 1), :].reshape(512, CELLS)
        turned = jnp.dot(swap, block, preferred_element_type=f32).astype(bf16)
        nat_ref[16 * g : 16 * (g + 1)] = turned.reshape(16, 32, CELLS)

    @pl.when(odd)
    def _():
        for side in range(2):
            drain(pair_ref.at[side], edge_sem.at[side])
            drain(ce_ref.at[side], coef_sem.at[side])

        drain(ch_ref, coef_sem.at[4])

    @pl.when(even)
    def _():
        for side in range(2):
            drain(pair_ref.at[side, pl.ds(0, 32)], pair_sem.at[side])

    outermost = (m == 0) | (m == GROUP - 1)

    @pl.when(outermost)
    def _():
        drain(r_ref.at[1, pl.ds(0, 32 * (GROUP - 2))], send_sem.at[0])

    @pl.when(jnp.logical_not(outermost))
    def _():
        drain(r_ref.at[1, pl.ds(0, 32 * (GROUP - 3))], send_sem.at[0])

    sent(4)
    forward.wait_send()
    for k in range(4):
        drain(out_ref.at[k, pl.ds(0, 32 * (GROUP - 1))], back_sem.at[k])
    for side, inside in ((0, d > 0), (1, d < count - 1)):

        @pl.when(inside)
        def _():
            drain(fe_ref.at[side], first_sem.at[1 - side])
            drain(fh_ref.at[side], first_sem.at[2 + side])
            halo_ref[side] = fh_ref[side]

        @pl.when(jnp.logical_not(inside))
        def _():
            halo_ref[side] = jnp.zeros((32, CELLS), f32)


STEP = 8


def correct_kernel(it_ref, src_ref, nat_ref, halo_ref, w_ref, inv_ref, upd_ref, res_ref):
    row = iota((32, CELLS), 0)

    def update(mode, _):
        res = src_ref[mode] - nat_ref[mode].astype(f32)
        res_ref[mode] = res
        first = res * inv_ref[0]
        total = it_ref[mode] + res * inv_ref[1]
        for f, amount in enumerate((CELLS - NZ, NZ, CELLS - 1, 1)):
            total = total + w_ref[2 + f] * pltpu.roll(first, amount, 1)
        above = jnp.where(row == 31, halo_ref[1, pl.ds(mode, 1), :], pltpu.roll(first, 31, 0))
        below = jnp.where(row == 0, halo_ref[0, pl.ds(mode, 1), :], pltpu.roll(first, 1, 0))
        upd_ref[mode] = total + w_ref[0] * above + w_ref[1] * below
        return 0

    lax.fori_loop(0, STEP, update, 0, unroll=4)


def body(iterate, source, mean_coef, kl_fields, tri_index, tri_value):
    sds = jax.ShapeDtypeStruct
    vm = pl.BlockSpec(memory_space=pltpu.VMEM)
    hbm = pl.BlockSpec(memory_space=pltpu.HBM)
    dma = pltpu.SemaphoreType.DMA
    natural, halo, w, inv = pl.pallas_call(
        exchange_kernel,
        out_shape=(
            sds((32, 32, CELLS), bf16),
            sds((2, 32, CELLS), f32),
            sds((6, 32, CELLS), f32),
            sds((2, 32, CELLS), f32),
        ),
        in_specs=[hbm] * 6,
        out_specs=(vm, vm, vm, vm),
        scratch_shapes=[
            pltpu.VMEM((32, 32, CELLS), f32),
            pltpu.VMEM((32, 32, CELLS), f32),
            pltpu.VMEM((32, CELLS), f32),
            pltpu.VMEM((NF - 1, 32, CELLS), f32),
            pltpu.VMEM((3, ENTRIES), i32),
            pltpu.VMEM((42, 128), f32),
            pltpu.VMEM((32, 32, CELLS), bf16),
            pltpu.VMEM((2, 64, CELLS), bf16),
            pltpu.VMEM((6, P_SIZE, CELLS), bf16),
            pltpu.VMEM((NIB, NF * IB, P_SIZE), bf16),
            pltpu.VMEM((P_SIZE, 64), f32),
            pltpu.VMEM((P_SIZE, CELLS), bf16),
            pltpu.VMEM((6, 24, CELLS), f32),
            pltpu.VMEM((4, 24, CELLS), f32),
            pltpu.VMEM((6, P_SIZE, CELLS), f32),
            pltpu.VMEM((4, P_SIZE, CELLS), f32),
            pltpu.VMEM((NF * IB, CELLS), f32),
            pltpu.VMEM((NF * IB, CELLS), f32),
            pltpu.VMEM((2, 24, CELLS), f32),
            pltpu.VMEM((2, 24, CELLS), f32),
            pltpu.VMEM((4, P_SIZE, CELLS), bf16),
            pltpu.VMEM((32, 32, CELLS), bf16),
            pltpu.VMEM((2, 32, CELLS), f32),
            pltpu.VMEM((2, 32, CELLS), f32),
            pltpu.VMEM((3, 32, CELLS), f32),
            dma((6,)),
            dma((2,)),
            dma((6,)),
            dma((6,)),
            dma((6,)),
            dma((4,)),
            dma((4,)),
            dma((4,)),
            dma((4,)),
            pltpu.SemaphoreType.REGULAR,
        ],
        compiler_params=pltpu.CompilerParams(
            collective_id=0, has_side_effects=True, vmem_limit_bytes=50 * 2**20
        ),
    )(*[
        pltpu.with_memory_space_constraint(x, pltpu.HBM)
        for x in (iterate, source, mean_coef, kl_fields, tri_index.T, tri_value.reshape(42, 128))
    ])

    big = pl.BlockSpec((STEP, 32, CELLS), lambda g: (g, 0, 0))
    return pl.pallas_call(
        correct_kernel,
        out_shape=(sds((32, 32, CELLS), f32), sds((32, 32, CELLS), f32)),
        grid=(32 // STEP,),
        in_specs=[
            big,
            big,
            big,
            pl.BlockSpec((2, STEP, CELLS), lambda g: (0, g, 0)),
            pl.BlockSpec((6, 32, CELLS), lambda g: (0, 0, 0)),
            pl.BlockSpec((2, 32, CELLS), lambda g: (0, 0, 0)),
        ],
        out_specs=(big, big),
        compiler_params=pltpu.CompilerParams(vmem_limit_bytes=16 * 2**20),
    )(iterate, source, natural, halo, w, inv)


def solution(mesh):
    return jax.shard_map(
        body,
        mesh=mesh,
        in_specs=(
            P("mode", "dom", None),
            P("mode", "dom", None),
            P("dom", None),
            P(None, "dom", None),
            P(),
            P(),
        ),
        out_specs=(P("mode", "dom", None), P("mode", "dom", None)),
        check_vma=False,
    )
```

```python
import jax
import jax.numpy as jnp
from jax import lax
from jax.experimental import pallas as pl
from jax.experimental.pallas import tpu as pltpu
from jax.sharding import PartitionSpec as P

P_SIZE = 256
NF = 21
NZ = 16
CELLS = 256
IB = 64
NIB = P_SIZE // IB
SUB = 16
PER = IB // 32
ENTRIES = P_SIZE * NF

cheb_center = 1.125
cheb_radius = 0.875
sigma = cheb_center / cheb_radius
rho_zero = 1.0 / sigma
rho_one = 1.0 / (2.0 * sigma - rho_zero)

f32 = jnp.float32
bf16 = jnp.bfloat16
i32 = jnp.int32


def iota(shape, dim):
    return lax.broadcasted_iota(i32, shape, dim)


def plane_neighbours():
    q = iota((CELLS, CELLS), 0)
    p = iota((CELLS, CELLS), 1)
    far = jnp.abs(q - p)
    same = (q >> 4) == (p >> 4)
    return jnp.where((far == NZ) | ((far == 1) & same), 1.0, 0.0).astype(bf16)


def fill_table(tri_ref, val_ref, table_ref):
    mode = iota((P_SIZE, 256), 0)
    level = iota((32, 256), 0)

    def gather(step, total):
        here = pl.ds(pl.multiple_of(step * 256, 256), 256)
        worth = jnp.concatenate([val_ref[pl.ds(2 * step, 1)], val_ref[pl.ds(2 * step + 1, 1)]], 1)
        hot = jnp.where(mode == tri_ref[0:1, here], 1.0, 0.0).astype(bf16)
        mine = level == tri_ref[2:3, here]
        coef = jnp.where(mine, worth, 0.0).astype(bf16)
        trial = jnp.where(mine, tri_ref[1:2, here].astype(f32), 0.0).astype(bf16)
        both = jnp.concatenate([coef, trial], 0)
        return total + lax.dot_general(
            hot, both, (((1,), (1,)), ((), ())), preferred_element_type=f32
        )

    table_ref[...] = lax.fori_loop(0, ENTRIES // 256, gather, jnp.zeros((P_SIZE, 64), f32))


def fill_mixing(table_ref, mix_ref):
    column = iota((P_SIZE, P_SIZE), 1).astype(f32)
    for l in range(NF):
        coef = table_ref[:, l : l + 1]
        trial = table_ref[:, 32 + l : 33 + l]
        panel = jnp.where(column == trial, coef, 0.0).astype(bf16)
        mix_ref[:, l * IB : (l + 1) * IB, :] = panel.reshape(NIB, IB, P_SIZE)


def swap_matrix(major, minor):
    n = major * minor
    r = iota((n, n), 0)
    c = iota((n, n), 1)
    shift = minor.bit_length() - 1
    wanted = (r & (minor - 1)) * major + (r >> shift)
    return jnp.where(c == wanted, 1.0, 0.0).astype(bf16)


def lane_neighbours(x, z_place, place):
    up = jnp.where(z_place < NZ - 1, pltpu.roll(x, CELLS - 1, x.ndim - 1), 0.0)
    down = jnp.where(z_place > 0, pltpu.roll(x, 1, x.ndim - 1), 0.0)
    far = jnp.where(place < CELLS - NZ, pltpu.roll(x, CELLS - NZ, x.ndim - 1), 0.0)
    near = jnp.where(place >= NZ, pltpu.roll(x, NZ, x.ndim - 1), 0.0)
    return up + down + far + near


def fill_faces(c0_ref, w_ref, inv_ref):
    place = iota((32, CELLS), 1)
    z_place = place & (NZ - 1)
    c = c0_ref[1]
    w_ref[0] = 0.5 * (c + c0_ref[2])
    w_ref[1] = 0.5 * (c + c0_ref[0])
    diag = w_ref[0] + w_ref[1]
    tests = ((CELLS - NZ, place < CELLS - NZ), (NZ, place >= NZ), (CELLS - 1, z_place < NZ - 1), (1, z_place > 0))
    for f, (amount, inside) in enumerate(tests):
        w = 0.5 * (c + jnp.where(inside, pltpu.roll(c, amount, 1), 0.0))
        diag = diag + w
        w_ref[2 + f] = jnp.where(inside, w, 0.0)
    inv = 1.0 / diag
    weight = (2.0 * rho_one / cheb_radius) * inv
    for f in range(6):
        w_ref[f] = w_ref[f] * weight
    inv_ref[0] = inv * (1.0 / cheb_center)
    inv_ref[1] = inv * ((1.0 + rho_one * rho_zero) / cheb_center) + weight * (1.0 - 1.0 / cheb_center)


MESH = pl.DeviceIdType.MESH
GROUP = 8


def row_of(device, k):
    core = lax.rem(device, 2)
    return 8 * (device // 2) + core * (8 - k) + (1 - core) * (k - 1)


def exchange_kernel(
    it_hbm, src_hbm, mean_hbm, kl_hbm, tri_hbm, val_hbm, upd_ref, res_ref,
    it_ref, src_ref, mean_ref, kl_ref, tri_ref, val_ref, rows_ref, pair_ref, r_ref, mix_ref, table_ref, g_ref, b_ref, nb_ref, s_ref, t_ref, u_ref, v_ref,
    ce_ref, ch_ref, out_ref, img_ref, fe_ref, fh_ref, c0_ref, w_ref, inv_ref,
    local_sem, edge_sem, send_sem, recv_sem, coef_sem, back_sem, home_sem, first_sem, pair_sem, go_sem,
):
    d = lax.axis_index("dom")
    m = lax.axis_index("mode")
    count = lax.axis_size("dom")
    up = lax.rem(d + 1, count)
    down = lax.rem(d + count - 1, count)
    sibling = m + 1 - 2 * lax.rem(m, 2)
    peers = [lax.rem(m + p, GROUP) for p in range(1, GROUP)]
    own_modes = pl.ds(pl.multiple_of(m * 32, 32), 32)

    def send(source, target, device, sent, got):
        copy = pltpu.make_async_remote_copy(
            src_ref=source, dst_ref=target, send_sem=sent, recv_sem=got, device_id=device, device_id_type=MESH
        )
        copy.start()
        return copy

    def drain(ref, sem):
        pltpu.make_async_copy(ref, ref, sem).wait()

    loads = [
        pltpu.make_async_copy(a, b, local_sem.at[i])
        for i, (a, b) in enumerate(
            (
                (it_hbm, it_ref),
                (kl_hbm, kl_ref),
                (mean_hbm, mean_ref),
                (tri_hbm, tri_ref),
                (val_hbm, val_ref),
                (src_hbm, src_ref),
            )
        )
    ]
    for load in loads:
        load.start()
    even = lax.rem(m, 2) == 0
    odd = lax.rem(m, 2) == 1
    barrier = pltpu.get_barrier_semaphore()
    for peer in peers:

        @pl.when(lax.rem(peer, 2) == 0)
        def _():
            pl.semaphore_signal(barrier, inc=1, device_id=(d, peer), device_id_type=MESH)

    @pl.when(odd)
    def _():
        for other in (up, down):
            pl.semaphore_signal(barrier, inc=1, device_id=(other, m), device_id_type=MESH)

    for holder, other in ((0, down), (GROUP - 1, up)):

        @pl.when(m == holder)
        def _():
            for q in range(1, GROUP, 2):
                pl.semaphore_signal(barrier, inc=1, device_id=(other, q), device_id_type=MESH)

    loads[0].wait()
    swap = swap_matrix(32, 16)
    for g in range(2):
        block = it_ref[16 * g : 16 * (g + 1)].astype(bf16).reshape(512, CELLS)
        turned = jnp.dot(swap, block, preferred_element_type=f32).astype(bf16)
        rows_ref[:, 16 * g : 16 * (g + 1), :] = turned.reshape(32, 16, CELLS)
    pair_ref[0, 32:64] = rows_ref[0]
    pair_ref[1, 32:64] = rows_ref[31]
    loads[1].wait()
    loads[2].wait()
    blank = jnp.zeros((3, CELLS), f32)
    for side, row in ((0, 0), (1, 31)):
        ce_ref[side] = jnp.concatenate([mean_ref[row : row + 1], kl_ref[:, row, :], blank], 0)

    @pl.when(even)
    def _():
        pl.semaphore_wait(barrier, GROUP - 1)
        pl.semaphore_signal(go_sem, inc=1, device_id=(d, sibling), device_id_type=MESH)

    @pl.when(odd)
    def _():
        pl.semaphore_wait(go_sem, 1)

    def issue(k):
        for peer in peers:
            row = row_of(peer, k)

            def pass_row():
                send(rows_ref.at[row], r_ref.at[k, own_modes], (d, peer), send_sem.at[k], recv_sem.at[k])

            if k > 0:
                pass_row()
            else:
                pl.when((row >= 0) & (row < 32))(pass_row)
        row = row_of(m, k)

        def keep_row():
            pltpu.make_async_copy(rows_ref.at[row], r_ref.at[k, own_modes], recv_sem.at[k]).start()

        if k > 0:
            keep_row()
        else:
            pl.when((row >= 0) & (row < 32))(keep_row)

    def sent(k):
        drain(r_ref.at[k, pl.ds(0, 32 * (GROUP - 1))], send_sem.at[k])

    @pl.when(even)
    def _():
        for side, row in ((0, 0), (1, 31)):
            send(rows_ref.at[row], pair_ref.at[side, pl.ds(0, 32)], (d, sibling), pair_sem.at[side], pair_sem.at[2 + side])

    issue(1)
    issue(2)
    loads[3].wait()
    loads[4].wait()
    fill_table(tri_ref, val_ref, table_ref)
    sent(1)
    issue(3)
    fill_mixing(table_ref, mix_ref)

    first_edge = jnp.where(d == 0, 0.0, 1.0)
    last_edge = jnp.where(d == count - 1, 0.0, 1.0)
    outer = jnp.where(m == 0, first_edge, jnp.where(m == GROUP - 1, last_edge, 1.0))

    def coef_row(row):
        kl_row = kl_ref[:, pl.ds(row, 1), :].reshape(NF - 1, CELLS)
        return jnp.concatenate([mean_ref[pl.ds(row, 1), :], kl_row, blank], 0)

    for k in range(1, 6):
        b_ref[k] = 0.5 * coef_row(row_of(m, k))
    place = iota((24, CELLS), 1)
    for k in range(1, 5):
        beside = b_ref[k + 1] if k == 1 else b_ref[k - 1] + b_ref[k + 1]
        nb_ref[k - 1] = beside + lane_neighbours(b_ref[k], place & (NZ - 1), place)
    near = plane_neighbours()
    sent(2)
    issue(4)

    def mixed(ib, panel, into):
        into[...] = jnp.dot(mix_ref[ib], panel, preferred_element_type=f32)

    def weigh(pairs, source, q, totals):
        totals = list(totals)
        for l in range(NF):
            piece = source[l * IB + q : l * IB + q + SUB]
            for n, coef in enumerate(pairs):
                term = coef[l : l + 1] * piece
                totals[n] = term if totals[n] is None else totals[n] + term
        return totals

    def take_plane(k):
        own = s_ref[k]
        high = own.astype(bf16)
        low = (own - high.astype(f32)).astype(bf16)
        around = jnp.dot(high, near, preferred_element_type=f32) + jnp.dot(low, near, preferred_element_type=f32)
        t_ref[k - 1] = t_ref[k - 1] - around

    def mix_slot(k):
        def block(ib, _):
            mixed(ib, r_ref[k], u_ref)
            for q in range(0, IB, SUB):
                here = pl.ds(pl.multiple_of(ib * IB + q, SUB), SUB)
                s_ref[k, here], t_ref[k - 1, here] = weigh((b_ref.at[k], nb_ref.at[k - 1]), u_ref, q, (None, None))
            return 0

        lax.fori_loop(0, NIB, block, 0)
        take_plane(k)

    def fill_differences(k):
        own = r_ref[k]
        behind = r_ref[k - 1].astype(f32)
        if k == 1:
            behind = behind * outer
            r_ref[0] = (own.astype(f32) - behind).astype(bf16)
        around = jnp.dot(own, near, preferred_element_type=f32)
        g_ref[...] = (6.0 * own.astype(f32) - around - behind - r_ref[k + 1].astype(f32)).astype(bf16)

    def finish_row(k):
        row = row_of(m, k)
        beside = 0 if k == 1 else k + 1
        other = 2 if k == 1 else k - 1

        def pass_on(device):
            modes = pl.ds(pl.multiple_of(device * 32, 32), 32)
            send(out_ref.at[k - 1, modes], img_ref.at[row], (d, device), back_sem.at[k - 1], home_sem.at[k - 1])

        def block(i, _):
            ib = lax.rem(m // PER + 1 + i, NIB)
            before = lax.rem(m // PER + i, NIB)

            @pl.when(i > 0)
            def _():
                for q in range(PER):
                    pass_on(PER * before + q)

            mixed(ib, r_ref[beside], u_ref)
            mixed(ib, g_ref[...], v_ref)
            for q in range(0, IB, SUB):
                here = pl.ds(pl.multiple_of(ib * IB + q, SUB), SUB)
                start = t_ref[k - 1, here] - s_ref[other, here]
                if beside in (3, 4):
                    sums, extra = weigh((b_ref.at[beside], nb_ref.at[beside - 1]), u_ref, q, (None, None))
                    s_ref[beside, here] = sums
                    t_ref[beside - 1, here] = extra
                else:
                    (sums,) = weigh((b_ref.at[beside],), u_ref, q, (None,))
                start = start + sums if k == 1 else start - sums
                (total,) = weigh((b_ref.at[k],), v_ref, q, (start,))
                out_ref[k - 1, here] = total.astype(bf16)
            return 0

        lax.fori_loop(0, NIB, block, 0)
        if beside in (3, 4):
            take_plane(beside)
        img_ref[row] = out_ref[k - 1, own_modes]

        def rest():
            for q in range(1, PER):
                pass_on(PER * (m // PER) + lax.rem(m + q, PER))

        return rest

    both_modes = pl.ds(pl.multiple_of((m // 2) * 64, 64), 64)
    seven = pl.ds(0, GROUP - 1)
    drain(r_ref.at[1], recv_sem.at[1])
    mix_slot(1)

    @pl.when(odd)
    def _():
        pl.semaphore_wait(barrier, 4)
        for side in range(2):
            drain(pair_ref.at[side, pl.ds(0, 32)], pair_sem.at[2 + side])
        send(pair_ref.at[1], r_ref.at[0, both_modes], (up, 0), edge_sem.at[0], recv_sem.at[0])
        send(pair_ref.at[0], r_ref.at[0, both_modes], (down, GROUP - 1), edge_sem.at[1], recv_sem.at[0])
        send(ce_ref.at[1], ch_ref.at[0], (up, m), coef_sem.at[0], coef_sem.at[2])
        send(ce_ref.at[0], ch_ref.at[1], (down, m), coef_sem.at[1], coef_sem.at[3])

    drain(r_ref.at[2], recv_sem.at[2])
    mix_slot(2)
    sent(3)
    issue(0)
    drain(r_ref.at[3], recv_sem.at[3])
    fill_differences(2)
    finish_row(2)()

    @pl.when(odd)
    def _():
        for side in range(2):
            drain(ch_ref.at[side], coef_sem.at[2 + side])
        send(ch_ref, ch_ref, (d, sibling), coef_sem.at[4], coef_sem.at[5])

    drain(r_ref.at[4], recv_sem.at[4])
    forward = send(r_ref.at[4], r_ref.at[5], (d, sibling), send_sem.at[5], recv_sem.at[5])
    fill_differences(3)
    finish_row(3)()

    @pl.when(even)
    def _():
        drain(ch_ref, coef_sem.at[5])

    row = row_of(m, 0)
    inside = coef_row(jnp.minimum(jnp.maximum(row, 0), 31))
    edge_coef = jnp.where(m == 0, ch_ref[0], jnp.where(m == GROUP - 1, ch_ref[1], inside))
    b_ref[0] = 0.5 * outer * edge_coef
    drain(r_ref.at[0], recv_sem.at[0])
    fill_differences(1)
    last = finish_row(1)

    row = iota((32, CELLS), 0)
    mean = mean_ref[...]
    c0_ref[0] = jnp.where(row == 0, ch_ref[0, 0:1] * first_edge, pltpu.roll(mean, 1, 0))
    c0_ref[1] = mean
    c0_ref[2] = jnp.where(row == 31, ch_ref[1, 0:1] * last_edge, pltpu.roll(mean, 31, 0))
    fill_faces(c0_ref, w_ref, inv_ref)
    last()
    forward.wait_recv()
    fill_differences(4)
    last = finish_row(4)
    loads[5].wait()
    last()
    drain(img_ref.at[seven], home_sem.at[0])
    first_inv = inv_ref[0]
    for side, row in ((0, 0), (1, 31)):
        fe_ref[side] = (src_ref[:, row, :] - img_ref[row].astype(f32)) * first_inv[row : row + 1]
    swap = swap_matrix(16, 32)
    @pl.when(d < count - 1)
    def _():
        send(fe_ref.at[1], fh_ref.at[0], (up, m), first_sem.at[0], first_sem.at[2])

    @pl.when(d > 0)
    def _():
        send(fe_ref.at[0], fh_ref.at[1], (down, m), first_sem.at[1], first_sem.at[3])

    for k in range(1, 4):
        drain(img_ref.at[seven], home_sem.at[k])
    for g in range(2):
        block = img_ref[:, 16 * g : 16 * (g + 1), :].reshape(512, CELLS)
        turned = jnp.dot(swap, block, preferred_element_type=f32).reshape(16, 32, CELLS)
        res_ref[16 * g : 16 * (g + 1)] = src_ref[16 * g : 16 * (g + 1)] - turned
    row = iota((32, CELLS), 0)

    def correct(mode, _):
        res = res_ref[mode]
        first = res * inv_ref[0]
        total = it_ref[mode] + res * inv_ref[1]
        for f, amount in enumerate((CELLS - NZ, NZ, CELLS - 1, 1)):
            total = total + w_ref[2 + f] * pltpu.roll(first, amount, 1)
        above = jnp.where(row == 31, 0.0, pltpu.roll(first, 31, 0))
        below = jnp.where(row == 0, 0.0, pltpu.roll(first, 1, 0))
        upd_ref[mode] = total + w_ref[0] * above + w_ref[1] * below
        return 0

    lax.fori_loop(0, 32, correct, 0, unroll=4)

    @pl.when(odd)
    def _():
        for side in range(2):
            drain(pair_ref.at[side], edge_sem.at[side])
            drain(ce_ref.at[side], coef_sem.at[side])

        drain(ch_ref, coef_sem.at[4])

    @pl.when(even)
    def _():
        for side in range(2):
            drain(pair_ref.at[side, pl.ds(0, 32)], pair_sem.at[side])

    outermost = (m == 0) | (m == GROUP - 1)

    @pl.when(outermost)
    def _():
        drain(r_ref.at[1, pl.ds(0, 32 * (GROUP - 2))], send_sem.at[0])

    @pl.when(jnp.logical_not(outermost))
    def _():
        drain(r_ref.at[1, pl.ds(0, 32 * (GROUP - 3))], send_sem.at[0])

    sent(4)
    forward.wait_send()
    for k in range(4):
        drain(out_ref.at[k, pl.ds(0, 32 * (GROUP - 1))], back_sem.at[k])
    for side, inside in ((0, d > 0), (1, d < count - 1)):

        @pl.when(inside)
        def _():
            drain(fe_ref.at[side], first_sem.at[1 - side])
            drain(fh_ref.at[side], first_sem.at[2 + side])
            edge = 31 * side
            weight = w_ref[1 - side, edge : edge + 1]
            upd_ref[:, edge, :] = upd_ref[:, edge, :] + weight * fh_ref[side]


def store_kernel(upd_ref, res_ref, upd_hbm, res_hbm, sem):
    copies = [
        pltpu.make_async_copy(a, b, sem.at[i]) for i, (a, b) in enumerate(((upd_ref, upd_hbm), (res_ref, res_hbm)))
    ]
    for copy in copies:
        copy.start()
    for copy in copies:
        copy.wait()


def body(iterate, source, mean_coef, kl_fields, tri_index, tri_value):
    sds = jax.ShapeDtypeStruct
    vm = pl.BlockSpec(memory_space=pltpu.VMEM)
    hbm = pl.BlockSpec(memory_space=pltpu.HBM)
    dma = pltpu.SemaphoreType.DMA
    block = sds((32, 32, CELLS), f32)
    updated, residual = pl.pallas_call(
        exchange_kernel,
        out_shape=(block, block),
        in_specs=[hbm] * 6,
        out_specs=(vm, vm),
        scratch_shapes=[
            pltpu.VMEM((32, 32, CELLS), f32),
            pltpu.VMEM((32, 32, CELLS), f32),
            pltpu.VMEM((32, CELLS), f32),
            pltpu.VMEM((NF - 1, 32, CELLS), f32),
            pltpu.VMEM((3, ENTRIES), i32),
            pltpu.VMEM((42, 128), f32),
            pltpu.VMEM((32, 32, CELLS), bf16),
            pltpu.VMEM((2, 64, CELLS), bf16),
            pltpu.VMEM((6, P_SIZE, CELLS), bf16),
            pltpu.VMEM((NIB, NF * IB, P_SIZE), bf16),
            pltpu.VMEM((P_SIZE, 64), f32),
            pltpu.VMEM((P_SIZE, CELLS), bf16),
            pltpu.VMEM((6, 24, CELLS), f32),
            pltpu.VMEM((4, 24, CELLS), f32),
            pltpu.VMEM((6, P_SIZE, CELLS), f32),
            pltpu.VMEM((4, P_SIZE, CELLS), f32),
            pltpu.VMEM((NF * IB, CELLS), f32),
            pltpu.VMEM((NF * IB, CELLS), f32),
            pltpu.VMEM((2, 24, CELLS), f32),
            pltpu.VMEM((2, 24, CELLS), f32),
            pltpu.VMEM((4, P_SIZE, CELLS), bf16),
            pltpu.VMEM((32, 32, CELLS), bf16),
            pltpu.VMEM((2, 32, CELLS), f32),
            pltpu.VMEM((2, 32, CELLS), f32),
            pltpu.VMEM((3, 32, CELLS), f32),
            pltpu.VMEM((6, 32, CELLS), f32),
            pltpu.VMEM((2, 32, CELLS), f32),
            dma((6,)),
            dma((2,)),
            dma((6,)),
            dma((6,)),
            dma((6,)),
            dma((4,)),
            dma((4,)),
            dma((4,)),
            dma((4,)),
            pltpu.SemaphoreType.REGULAR,
        ],
        compiler_params=pltpu.CompilerParams(
            collective_id=0, has_side_effects=True, vmem_limit_bytes=50 * 2**20
        ),
    )(*[
        pltpu.with_memory_space_constraint(x, pltpu.HBM)
        for x in (iterate, source, mean_coef, kl_fields, tri_index.T, tri_value.reshape(42, 128))
    ])

    return pl.pallas_call(
        store_kernel,
        out_shape=(block, block),
        in_specs=[vm, vm],
        out_specs=(pl.BlockSpec(memory_space=pl.ANY),) * 2,
        scratch_shapes=[dma((2,))],
        compiler_params=pltpu.CompilerParams(vmem_limit_bytes=8 * 2**20),
    )(updated, residual)


def solution(mesh):
    return jax.shard_map(
        body,
        mesh=mesh,
        in_specs=(
            P("mode", "dom", None),
            P("mode", "dom", None),
            P("dom", None),
            P(None, "dom", None),
            P(),
            P(),
        ),
        out_specs=(P("mode", "dom", None), P("mode", "dom", None)),
        check_vma=False,
    )
```
